128 devices in a mesh: slab: 8 (over z, core), sector: 16 (over y, x).
Axes of the slice: x: 4, y: 4, z: 4, core: 2. Of those that a mesh axis runs over, the one named last changes fastest.
Arguments:
- sources: bfloat16 [524288, 128], P(('slab', 'sector')), may hold values from -6 to 6
- bases: bfloat16 [2048, 256, 64], P(('slab', 'sector')), may hold values from -0.375 to 0.375
- leaf_parent: int32 [2048], P(('slab', 'sector')), may hold values from 0 to 1023, as said below
- up_transfer: float32 [2048, 64, 64], P(('slab', 'sector')), may hold values from -0.5 to 0.5
- root_transfer: float32 [1024, 64, 64], P(('slab', 'sector')), may hold values from -0.25 to 0.25
- top_transfer: float32 [256, 64, 64], replicated, may hold values from -0.75 to 0.75
- top_coupling: float32 [256, 64, 64], replicated, may hold values from -0.75 to 0.75
- near_list: int32 [2048, 8], P(('slab', 'sector')), may hold values from 0 to 2047, as said below
- near_blocks: bfloat16 [2048, 8, 256, 256], P(('slab', 'sector')), may hold values from -0.125 to 0.125
- far_list: int32 [2048, 16], P(('slab', 'sector')), may hold values from 0 to 2047, as said below
- far_count: int32 [2048], P(('slab', 'sector')), may hold values from 1 to 16, as said below
- far_coupling: float32 [2048, 16, 64, 64], P(('slab', 'sector')), may hold values from -0.1875 to 0.1875
Outputs:
- field: bfloat16 [524288, 128], P(('slab', 'sector'))
The draws below stay inside these ranges and needn't reach their ends.
Inputs may be any that keep to these rules, and one draw needn't show every extreme that they name: leaf_parent pairs the leaves of each device d: every cluster d * 8 to (d + 1) * 8 - 1 is the parent of exactly two of device d's leaves. `near_list`: each entry is a leaf on the same device or on a device at most one slab and at most one sector away, sectors counted around the cycle. `far_list`: each entry is a leaf of the same slab. `far_count`: some leaf uses all 16 slots.
All inputs are finite; a program needn't handle non-finite values.
Results may differ from the reference program's by a relative error of at most 0.0085.
Values may be sent and summed in bfloat16 or wider, within the bound.
No kernel may reach another device: no remote copies, remote signals or barrier semaphores. Data moves between devices by JAX's collectives and lax.ppermute only.
A program may use at most 256 MiB of HBM per device.

```python
import jax
import jax.numpy as jnp
from jax import lax

LEAF = 256
RANK = 64
RHS = 128
L_DEV = 16
NEAR = 8
FAR0 = 16
LEAVES = 2048
CLUSTERS = 1024
PANELS = 524288
NODES = 256
N_SLAB = 8
N_SECTOR = 16


def draw_leaf_parent(key, part):
    devices = N_SLAB * N_SECTOR
    device_keys = jax.random.split(key, devices)
    shuffled = jax.vmap(lambda one_key: jax.random.permutation(one_key, L_DEV))(device_keys)
    offsets = jnp.arange(devices, dtype=jnp.int32)[:, None] * (L_DEV // 2)
    return (offsets + shuffled.astype(jnp.int32) // 2).reshape(-1).astype(jnp.int32)


def draw_near_list(key, part):
    devices = N_SLAB * N_SECTOR
    leaves = devices * L_DEV
    first_key, second_key = jax.random.split(jax.random.fold_in(key, 11))
    opening = jax.random.randint(first_key, (leaves, 1), 0, 9)
    offset_code = (opening + jnp.arange(NEAR, dtype=jnp.int32)[None, :]) % 9
    slab_step = offset_code // 3 - 1
    sector_step = offset_code % 3 - 1
    owners = jnp.arange(leaves, dtype=jnp.int32) // L_DEV
    own_slab = (owners // N_SECTOR)[:, None]
    own_sector = (owners % N_SECTOR)[:, None]
    target_slab = own_slab + slab_step
    target_slab = jnp.where((target_slab < 0) | (target_slab >= N_SLAB), own_slab - slab_step, target_slab)
    target_sector = (own_sector + sector_step) % N_SECTOR
    within = jax.random.randint(second_key, (leaves, NEAR), 0, L_DEV)
    return ((target_slab * N_SECTOR + target_sector) * L_DEV + within).astype(jnp.int32)


def draw_far_list(key, part):
    devices = N_SLAB * N_SECTOR
    leaves = devices * L_DEV
    owners = jnp.arange(leaves, dtype=jnp.int32) // L_DEV
    slab_start = owners // N_SECTOR * (N_SECTOR * L_DEV)
    chosen = jax.random.randint(jax.random.fold_in(key, 23), (leaves, FAR0), 0, N_SECTOR * L_DEV)
    return (slab_start[:, None] + chosen).astype(jnp.int32)


def draw_far_count(key, part):
    leaves = N_SLAB * N_SECTOR * L_DEV
    first_key, second_key = jax.random.split(jax.random.fold_in(key, 37))
    counts = jax.random.randint(first_key, (leaves,), 1, FAR0 + 1)
    fullest = jax.random.randint(second_key, (), 0, leaves)
    counts = jnp.where(jnp.arange(leaves, dtype=jnp.int32) == fullest, FAR0, counts)
    return counts.astype(jnp.int32)


def block_levels(key, extent, cuts, least, top_value):
    gain, own = 1.0, jax.random.fold_in(key, 6)
    for dim, shards_of in cuts:
        draws = jnp.exp(jax.random.uniform(jax.random.fold_in(own, dim), (shards_of,), jnp.float32, least / len(cuts), top_value / len(cuts)))
        gain = gain * jnp.repeat(draws, extent[dim] // shards_of).reshape([-1 if axis == dim else 1 for axis in range(len(extent))])
    return gain


def bell_draw(key, shape, width, reach, cuts=(), kind=jnp.bfloat16):
    level = block_levels(key, shape, cuts, -0.22, 0.18) if cuts else 1.0
    values = jax.random.normal(key, shape, jnp.float32) * width * level
    return jnp.minimum(jnp.maximum(values, -reach), reach).astype(kind)


def setup_inputs(seed: int = 0) -> dict:
    arg_keys = jax.random.split(jax.random.key(seed), 13)
    return {
        "sources": bell_draw(arg_keys[0], (PANELS, RHS), 1.0, 6.0, ((0, 128),)),
        "bases": bell_draw(arg_keys[1], (LEAVES, LEAF, RANK), LEAF ** -0.5, 0.375, ((0, 128),)),
        "leaf_parent": draw_leaf_parent(jax.random.fold_in(arg_keys[12], 71), 0),
        "up_transfer": bell_draw(arg_keys[3], (LEAVES, RANK, RANK), (2 * RANK) ** -0.5, 0.5, ((0, 128),), jnp.float32),
        "root_transfer": bell_draw(arg_keys[4], (CLUSTERS, RANK, RANK), (RANK * L_DEV // 2) ** -0.5, 0.25, ((0, 128),), jnp.float32),
        "top_transfer": bell_draw(arg_keys[5], (NODES, RANK, RANK), RANK ** -0.5, 0.75, (), jnp.float32),
        "top_coupling": bell_draw(arg_keys[6], (NODES, RANK, RANK), RANK ** -0.5, 0.75, (), jnp.float32),
        "near_list": draw_near_list(jax.random.fold_in(arg_keys[12], 71), 0),
        "near_blocks": bell_draw(arg_keys[8], (LEAVES, NEAR, LEAF, LEAF), (LEAF * NEAR) ** -0.5, 0.125, ((0, 128),)),
        "far_list": draw_far_list(jax.random.fold_in(arg_keys[12], 71), 0),
        "far_count": draw_far_count(jax.random.fold_in(arg_keys[12], 71), 0),
        "far_coupling": bell_draw(arg_keys[11], (LEAVES, FAR0, RANK, RANK), (RANK * FAR0) ** -0.5, 0.1875, ((0, 128),), jnp.float32),
    }


highest = lax.Precision.HIGHEST


def reference(sources, bases, leaf_parent, up_transfer, root_transfer, top_transfer, top_coupling, near_list, near_blocks, far_list, far_count, far_coupling):
    leaves = bases.shape[0]
    clusters = leaves // 2
    devices = N_SLAB * N_SECTOR
    per_device = clusters // devices
    panels = sources.reshape(leaves, LEAF, RHS)
    leaf_coefs = jnp.einsum("lpk,lpr->lkr", bases.astype(jnp.float32), panels.astype(jnp.float32), precision=highest)
    lifted = jnp.einsum("lkj,lkr->ljr", up_transfer, leaf_coefs, precision=highest)
    member = (leaf_parent[:, None] == jnp.arange(clusters, dtype=jnp.int32)[None, :]).astype(jnp.float32)
    cluster_coefs = jnp.einsum("lc,ljr->cjr", member, lifted, precision=highest)
    raised = jnp.einsum("ckj,ckr->cjr", root_transfer, cluster_coefs, precision=highest)
    current = jnp.sum(raised.reshape(devices, per_device, RANK, RHS), axis=1)
    depth = devices.bit_length() - 1
    coupled = []
    for level in range(depth):
        nodes_now = devices >> level
        siblings = current.reshape(nodes_now // 2, 2, RANK, RHS)[:, ::-1].reshape(nodes_now, RANK, RHS)
        coupled.append(jnp.einsum("gij,gjr->gir", top_coupling[nodes_now:2 * nodes_now], siblings, precision=highest))
        upward = jnp.einsum("gkj,gkr->gjr", top_transfer[nodes_now:2 * nodes_now], current, precision=highest)
        upward = upward.reshape(nodes_now // 2, 2, RANK, RHS)
        current = upward[:, 0] + upward[:, 1]
    downward = jnp.zeros((1, RANK, RHS), jnp.float32)
    for level in reversed(range(depth)):
        nodes_now = devices >> level
        parents = jnp.repeat(downward, 2, axis=0)
        downward = coupled[level] + jnp.einsum("gkj,gjr->gkr", top_transfer[nodes_now:2 * nodes_now], parents, precision=highest)
    on_cluster = jnp.einsum("ckj,cjr->ckr", root_transfer, jnp.repeat(downward, per_device, axis=0), precision=highest)
    on_leaf = jnp.einsum("lkj,ljr->lkr", up_transfer, on_cluster[leaf_parent], precision=highest)
    slot_ids = jnp.arange(FAR0, dtype=jnp.int32)

    def one_leaf(items):
        near_ids, blocks, far_ids, live, couplings = items
        picked = panels[near_ids].astype(jnp.float32)
        near_part = jnp.einsum("nij,njr->ir", blocks.astype(jnp.float32), picked, precision=highest)
        weights = couplings * (slot_ids < live).astype(jnp.float32)[:, None, None]
        far_part = jnp.einsum("fij,fjr->ir", weights, leaf_coefs[far_ids], precision=highest)
        return near_part, far_part

    near_field, far_field = lax.map(one_leaf, (near_list, near_blocks, far_list, far_count, far_coupling))
    expansion = (on_leaf + far_field).astype(jnp.bfloat16)
    expansion = lax.optimization_barrier(expansion)
    field = jnp.einsum("lpk,lkr->lpr", bases.astype(jnp.float32), expansion.astype(jnp.float32), precision=highest) + near_field
    return field.astype(jnp.bfloat16).reshape(leaves * LEAF, RHS)
```

```python
import jax
import jax.numpy as jnp
from jax import lax
from jax.experimental import pallas as pl
from jax.experimental.pallas import tpu as pltpu
from jax.sharding import PartitionSpec as P

highest = lax.Precision.HIGHEST
f32 = jnp.float32
bf16 = jnp.bfloat16


def dot_t(a, b, precision=None):
    return lax.dot_general(a, b, (((0,), (0,)), ((), ())), precision=precision, preferred_element_type=f32)


def dot(a, b, precision=None):
    return lax.dot_general(a, b, (((1,), (0,)), ((), ())), precision=precision, preferred_element_type=f32)


def whole():
    return pl.BlockSpec(memory_space=pltpu.VMEM)


def scalars():
    return pl.BlockSpec(memory_space=pltpu.SMEM)


def params(mib, semantics=None):
    return pltpu.CompilerParams(vmem_limit_bytes=mib << 20, dimension_semantics=semantics)


def cost(flops, nbytes):
    return pl.CostEstimate(flops=flops, bytes_accessed=nbytes, transcendentals=0)


def upward_kernel(parent, sources, bases, up, root, leaf_out, root_out, clusters):
    clusters[...] = jnp.zeros_like(clusters)
    for leaf in range(bases.shape[0]):
        coefs = dot_t(bases[leaf], sources[leaf])
        leaf_out[leaf] = coefs.astype(bf16)
        clusters[parent[leaf]] += dot_t(up[leaf], coefs, highest)
    total = dot_t(root[0], clusters[0], highest)
    for cluster in range(1, root.shape[0]):
        total = total + dot_t(root[cluster], clusters[cluster], highest)
    root_out[...] = total


def upward(local_parent, panels, bases, up_transfer, root_transfer):
    leaves, _, rhs = panels.shape
    rank = bases.shape[2]
    return pl.pallas_call(
        upward_kernel,
        out_shape=(
            jax.ShapeDtypeStruct((leaves, rank, rhs), bf16),
            jax.ShapeDtypeStruct((rank, rhs), f32),
        ),
        in_specs=[scalars(), whole(), whole(), whole(), whole()],
        out_specs=(whole(), whole()),
        scratch_shapes=[pltpu.VMEM((root_transfer.shape[0], rank, rhs), f32)],
        compiler_params=params(16),
        cost_estimate=cost(200_000_000, 4_000_000),
        name="upward",
    )(local_parent, panels, bases, up_transfer, root_transfer)


def tables_kernel(nodes, transfer, coupling, out, sems):
    depth = out.shape[0] // 3
    copies = []
    for level in range(depth):
        for kind in range(3):
            slot = 3 * level + kind
            table = coupling if kind == 2 else transfer
            node = nodes[level] ^ 1 if kind == 1 else nodes[level]
            copies.append(pltpu.make_async_copy(table.at[node], out.at[slot], sems.at[slot]))
    for copy in copies:
        copy.start()
    for copy in copies:
        copy.wait()


def tables(nodes, transfer, coupling):
    count = 3 * nodes.shape[0]
    return pl.pallas_call(
        tables_kernel,
        out_shape=jax.ShapeDtypeStruct((count,) + transfer.shape[1:], f32),
        in_specs=[scalars(), pl.BlockSpec(memory_space=pl.ANY), pl.BlockSpec(memory_space=pl.ANY)],
        out_specs=whole(),
        scratch_shapes=[pltpu.SemaphoreType.DMA((count,))],
        compiler_params=params(4),
        cost_estimate=cost(0, 700_000),
        name="tables",
    )(nodes, transfer, coupling)


def combine_kernel(level, current, sibling, mats, out):
    own = dot_t(mats[3 * level], current[...], highest)
    out[...] = own + dot_t(mats[3 * level + 1], sibling[...], highest)


def combine(level, current, sibling, mats):
    return pl.pallas_call(
        lambda *refs: combine_kernel(level, *refs),
        out_shape=jax.ShapeDtypeStruct(current.shape, f32),
        in_specs=[whole(), whole(), whole()],
        out_specs=whole(),
        compiler_params=params(4),
        cost_estimate=cost(12_000_000, 100_000),
        name="combine",
    )(current, sibling, mats)


def downward_kernel(depth, parent, *refs):
    siblings = refs[:depth]
    mats, root, up, out, clusters = refs[depth:]
    down = dot(mats[3 * depth - 1], siblings[depth - 1][...], highest)
    for level in reversed(range(depth - 1)):
        across = dot(mats[3 * level + 2], siblings[level][...], highest)
        down = across + dot(mats[3 * level], down, highest)
    for cluster in range(root.shape[0]):
        clusters[cluster] = dot(root[cluster], down, highest)
    for leaf in range(up.shape[0]):
        out[leaf] = dot(up[leaf], clusters[parent[leaf]], highest)


def downward(local_parent, siblings, mats, root_transfer, up_transfer):
    depth = len(siblings)
    rank, rhs = siblings[0].shape
    return pl.pallas_call(
        lambda *refs: downward_kernel(depth, *refs),
        out_shape=jax.ShapeDtypeStruct((up_transfer.shape[0], rank, rhs), f32),
        in_specs=[scalars()] + [whole()] * (depth + 3),
        out_specs=whole(),
        scratch_shapes=[pltpu.VMEM((root_transfer.shape[0], rank, rhs), f32)],
        compiler_params=params(16),
        cost_estimate=cost(200_000_000, 2_000_000),
        name="downward",
    )(local_parent, *siblings, mats, root_transfer, up_transfer)


def weights_kernel(count, coupling, out):
    leaf = pl.program_id(0)
    used = count[leaf]
    for pair in range(coupling.shape[1] // 2):
        left = jnp.where(2 * pair < used, coupling[0, 2 * pair], 0.0)
        right = jnp.where(2 * pair + 1 < used, coupling[0, 2 * pair + 1], 0.0)
        width = 2 * coupling.shape[3]
        out[0, :, pair * width : (pair + 1) * width] = jnp.concatenate([left, right], axis=1).astype(bf16)


def weights(far_count, far_coupling):
    leaves, slots, rank, _ = far_coupling.shape
    return pl.pallas_call(
        weights_kernel,
        out_shape=jax.ShapeDtypeStruct((leaves, rank, slots * rank), bf16),
        grid_spec=pltpu.PrefetchScalarGridSpec(
            num_scalar_prefetch=1,
            grid=(leaves,),
            in_specs=[pl.BlockSpec((1, slots, rank, rank), lambda i, n: (i, 0, 0, 0))],
            out_specs=pl.BlockSpec((1, rank, slots * rank), lambda i, n: (i, 0, 0)),
        ),
        compiler_params=params(8, ("arbitrary",)),
        cost_estimate=cost(0, 11_000_000),
        name="weights",
    )(far_count, far_coupling)


def near_kernel(position, blocks, *refs):
    regions = refs[:9]
    out, held, sems = refs[9:]
    leaves = regions[0].shape[0]
    leaf = pl.program_id(0)

    @pl.when(leaf == 0)
    def _():
        copies = [
            pltpu.make_async_copy(region, held.at[pl.ds(place * leaves, leaves)], sems.at[place])
            for place, region in enumerate(regions)
        ]
        for copy in copies:
            copy.start()
        for copy in copies:
            copy.wait()

    slots = blocks.shape[1]
    total = dot(blocks[0, 0], held[position[leaf * slots]])
    for slot in range(1, slots):
        total = total + dot(blocks[0, slot], held[position[leaf * slots + slot]])
    out[0] = total


def near(position, near_blocks, regions):
    leaves, slots, size, _ = near_blocks.shape
    rhs = regions[0].shape[2]
    return pl.pallas_call(
        near_kernel,
        out_shape=jax.ShapeDtypeStruct((leaves, size, rhs), f32),
        grid_spec=pltpu.PrefetchScalarGridSpec(
            num_scalar_prefetch=1,
            grid=(leaves,),
            in_specs=[pl.BlockSpec((1, slots, size, size), lambda i, p: (i, 0, 0, 0))]
            + [pl.BlockSpec(memory_space=pl.ANY)] * 9,
            out_specs=pl.BlockSpec((1, size, rhs), lambda i, p: (i, 0, 0)),
            scratch_shapes=[pltpu.VMEM((9 * leaves, size, rhs), bf16), pltpu.SemaphoreType.DMA((9,))],
        ),
        compiler_params=params(24, ("arbitrary",)),
        cost_estimate=cost(2_200_000_000, 28_000_000),
        name="near",
    )(position, near_blocks, *regions)


def final_kernel(rows, packed, coefs, on_leaf, bases, near_part, out, picked):
    leaf = pl.program_id(0)
    rank = coefs.shape[1]
    slots = packed.shape[2] // rank
    for slot in range(slots):
        picked[slot * rank : (slot + 1) * rank] = coefs[rows[leaf * slots + slot]]
    expansion = (on_leaf[0] + dot(packed[0], picked[...])).astype(bf16)
    out[0] = (dot(bases[0], expansion) + near_part[0]).astype(bf16)


def final(far_rows, packed, slab_coefs, on_leaf, bases, near_part):
    leaves, size, rank = bases.shape
    rhs = near_part.shape[2]
    wide = packed.shape[2]
    return pl.pallas_call(
        final_kernel,
        out_shape=jax.ShapeDtypeStruct((leaves, size, rhs), bf16),
        grid_spec=pltpu.PrefetchScalarGridSpec(
            num_scalar_prefetch=1,
            grid=(leaves,),
            in_specs=[
                pl.BlockSpec((1, rank, wide), lambda i, r: (i, 0, 0)),
                pl.BlockSpec(slab_coefs.shape, lambda i, r: (0, 0, 0), pipeline_mode=pl.Buffered(1)),
                pl.BlockSpec((1, rank, rhs), lambda i, r: (i, 0, 0)),
                pl.BlockSpec((1, size, rank), lambda i, r: (i, 0, 0)),
                pl.BlockSpec((1, size, rhs), lambda i, r: (i, 0, 0)),
            ],
            out_specs=pl.BlockSpec((1, size, rhs), lambda i, r: (i, 0, 0)),
            scratch_shapes=[pltpu.VMEM((wide, rhs), bf16)],
        ),
        compiler_params=params(16, ("arbitrary",)),
        cost_estimate=cost(350_000_000, 12_000_000),
        name="final",
    )(far_rows, packed, slab_coefs, on_leaf, bases, near_part)


def shifted(array, axis, step, closed):
    count = lax.axis_size(axis)
    pairs = [(i, (i + step) % count) for i in range(count) if closed or 0 <= i + step < count]
    return lax.ppermute(array, axis, pairs)


def partner(array, axis, stride):
    return lax.ppermute(array, axis, [(i, i ^ 1 << stride) for i in range(lax.axis_size(axis))])


def local(
    sources,
    bases,
    leaf_parent,
    up_transfer,
    root_transfer,
    top_transfer,
    top_coupling,
    near_list,
    near_blocks,
    far_list,
    far_count,
    far_coupling,
):
    leaf_total, leaf_size, _ = bases.shape
    rhs_count = sources.shape[1]
    cluster_total = leaf_total // 2
    slab_count = lax.axis_size("slab")
    sector_count = lax.axis_size("sector")
    devices = slab_count * sector_count
    depth = devices.bit_length() - 1
    slab_pos = lax.axis_index("slab")
    sector_pos = lax.axis_index("sector")
    device = slab_pos * sector_count + sector_pos
    panels = sources.reshape(leaf_total, leaf_size, rhs_count)

    before, after = shifted(panels, "sector", 1, True), shifted(panels, "sector", -1, True)
    regions = [before, panels, after]
    below = [shifted(region, "slab", 1, False) for region in regions]
    above = [shifted(region, "slab", -1, False) for region in regions]
    regions = below + regions + above

    local_parent = leaf_parent - device * cluster_total
    leaf_coefs, current = upward(local_parent, panels, bases, up_transfer, root_transfer)
    slab_coefs = lax.all_gather(leaf_coefs, "sector", axis=0, tiled=True)
    levels = jnp.arange(depth, dtype=jnp.int32)
    mats = tables((devices + device) >> levels, top_transfer, top_coupling)
    siblings = []
    for level in range(depth):
        siblings.append(partner(current, ("slab", "sector"), level))
        if level < depth - 1:
            current = combine(level, current, siblings[-1], mats)
    on_leaf = downward(local_parent, siblings, mats, root_transfer, up_transfer)

    packed = weights(far_count, far_coupling)

    owner_device = near_list // leaf_total
    slab_offset = owner_device // sector_count - slab_pos + 1
    sector_offset = (owner_device % sector_count - sector_pos + 1) % sector_count
    position = (slab_offset * 3 + sector_offset) * leaf_total + near_list % leaf_total
    near_part = near(position.reshape(-1), near_blocks, regions)

    far_rows = (far_list - slab_pos * (sector_count * leaf_total)).reshape(-1)
    field = final(far_rows, packed, slab_coefs, on_leaf, bases, near_part)
    return field.reshape(leaf_total * leaf_size, rhs_count)


def solution(mesh):
    placed = (
        P(("slab", "sector"), None),
        P(("slab", "sector"), None, None),
        P(("slab", "sector")),
        P(("slab", "sector"), None, None),
        P(("slab", "sector"), None, None),
        P(),
        P(),
        P(("slab", "sector"), None),
        P(("slab", "sector"), None, None, None),
        P(("slab", "sector"), None),
        P(("slab", "sector")),
        P(("slab", "sector"), None, None, None),
    )
    return jax.shard_map(
        local, mesh=mesh, in_specs=placed, out_specs=P(("slab", "sector"), None), check_vma=False
    )
```

```python
import jax
import jax.numpy as jnp
from jax import lax
from jax.experimental import pallas as pl
from jax.experimental.pallas import tpu as pltpu
from jax.sharding import PartitionSpec as P

highest = lax.Precision.HIGHEST
f32 = jnp.float32
bf16 = jnp.bfloat16


def dot_t(a, b, precision=None):
    return lax.dot_general(a, b, (((0,), (0,)), ((), ())), precision=precision, preferred_element_type=f32)


def dot(a, b, precision=None):
    return lax.dot_general(a, b, (((1,), (0,)), ((), ())), precision=precision, preferred_element_type=f32)


def dot_r(a, b):
    return lax.dot_general(a, b, (((1,), (1,)), ((), ())), preferred_element_type=f32)


def in_hbm(array):
    return pltpu.with_memory_space_constraint(array, pltpu.HBM)


def whole():
    return pl.BlockSpec(memory_space=pltpu.VMEM)


def anywhere():
    return pl.BlockSpec(memory_space=pl.ANY)


def scalars():
    return pl.BlockSpec(memory_space=pltpu.SMEM)


def params(mib, semantics=None):
    return pltpu.CompilerParams(vmem_limit_bytes=mib << 20, dimension_semantics=semantics)


def cost(flops, nbytes):
    return pl.CostEstimate(flops=flops, bytes_accessed=nbytes, transcendentals=0)


def coefs_kernel(sources, bases, leaf_out, held, basis, sems):
    group = sems.shape[0]
    step = held.shape[0] // group
    copies = []
    for part in range(group):
        rows = pl.ds(part * step, step)
        copies.append(
            (
                pltpu.make_async_copy(sources.at[rows], held.at[rows], sems.at[part, 0]),
                pltpu.make_async_copy(bases.at[rows], basis.at[rows], sems.at[part, 1]),
            )
        )
    for pair in copies:
        for copy in pair:
            copy.start()
    for part, pair in enumerate(copies):
        for copy in pair:
            copy.wait()
        for leaf in range(part * step, (part + 1) * step):
            leaf_out[leaf] = dot(basis[leaf], held[leaf]).astype(bf16)


def leaf_coefficients(panels, bases):
    leaves, size, rhs = panels.shape
    rank = bases.shape[1]
    return pl.pallas_call(
        coefs_kernel,
        out_shape=jax.ShapeDtypeStruct((leaves, rank, rhs), bf16),
        in_specs=[anywhere(), anywhere()],
        out_specs=whole(),
        scratch_shapes=[
            pltpu.VMEM((leaves, size, rhs), bf16),
            pltpu.VMEM((leaves, rank, size), bf16),
            pltpu.SemaphoreType.DMA((4, 2)),
        ],
        compiler_params=params(8),
        cost_estimate=cost(1000, 1000),
        name="coefs",
    )(in_hbm(panels), in_hbm(bases))


def upward_kernel(parent, coefs, up, root, root_out, clusters):
    clusters[...] = jnp.zeros_like(clusters)
    for leaf in range(coefs.shape[0]):
        clusters[parent[leaf]] += dot_t(up[leaf], coefs[leaf].astype(f32), highest)
    total = dot_t(root[0], clusters[0], highest)
    for cluster in range(1, root.shape[0]):
        total = total + dot_t(root[cluster], clusters[cluster], highest)
    root_out[...] = total


def upward(local_parent, leaf_coefs, up_transfer, root_transfer):
    leaves, rank, rhs = leaf_coefs.shape
    return pl.pallas_call(
        upward_kernel,
        out_shape=jax.ShapeDtypeStruct((rank, rhs), f32),
        in_specs=[scalars(), whole(), whole(), whole()],
        out_specs=whole(),
        scratch_shapes=[pltpu.VMEM((root_transfer.shape[0], rank, rhs), f32)],
        compiler_params=params(8),
        cost_estimate=cost(1000, 1000),
        name="upward",
    )(local_parent, leaf_coefs, up_transfer, root_transfer)


def tables_kernel(nodes, *refs):
    half = len(refs) // 2
    rank, size = refs[0].shape[1:]
    ids = lax.broadcasted_iota(jnp.int32, (nodes.shape[0], size), 1)
    chosen = (ids == nodes[...]).astype(bf16)
    for table, out in zip(refs[:half], refs[half:]):
        values = table[...].reshape(-1, size)
        high = values.astype(bf16)
        low = (values - high.astype(f32)).astype(bf16)
        rows = dot_r(chosen, high) + dot_r(chosen, low)
        for row in range(table.shape[0]):
            out[:, row, :] = rows[:, row * rank : (row + 1) * rank]


def tables(nodes, transfer, coupling):
    count = nodes.shape[0]
    size, rank, _ = transfer.shape
    step = 16
    return pl.pallas_call(
        tables_kernel,
        out_shape=(jax.ShapeDtypeStruct((count, rank, rank), f32),) * 2,
        grid=(rank // step,),
        in_specs=[pl.BlockSpec((count, 1), lambda i: (0, 0))]
        + [pl.BlockSpec((step, rank, size), lambda i: (i, 0, 0))] * 2,
        out_specs=(pl.BlockSpec((count, step, rank), lambda i: (0, i, 0)),) * 2,
        compiler_params=params(16, ("arbitrary",)),
        cost_estimate=cost(1000, 1000),
        name="tables",
    )(nodes, in_hbm(transfer.transpose(1, 2, 0)), in_hbm(coupling.transpose(1, 2, 0)))


def combine_kernel(own, other, current, sibling, mats, out):
    total = dot_t(mats[own], current[...], highest)
    out[...] = total + dot_t(mats[other], sibling[...], highest)


def combine(own, other, current, sibling, mats):
    return pl.pallas_call(
        lambda *refs: combine_kernel(own, other, *refs),
        out_shape=jax.ShapeDtypeStruct(current.shape, f32),
        in_specs=[whole(), whole(), whole()],
        out_specs=whole(),
        compiler_params=params(4),
        cost_estimate=cost(1000, 1000),
        name="combine",
    )(current, sibling, mats)


def downward_kernel(depth, parent, *refs):
    siblings = refs[:depth]
    transfer, coupling, root, up, out, clusters = refs[depth:]
    down = dot(coupling[depth - 1], siblings[depth - 1][...], highest)
    for level in reversed(range(depth - 1)):
        across = dot(coupling[level], siblings[level][...], highest)
        down = across + dot(transfer[level], down, highest)
    for cluster in range(root.shape[0]):
        clusters[cluster] = dot(root[cluster], down, highest)
    for leaf in range(up.shape[0]):
        out[leaf] = dot(up[leaf], clusters[parent[leaf]], highest)


def downward(local_parent, siblings, transfer, coupling, root_transfer, up_transfer):
    depth = len(siblings)
    rank, rhs = siblings[0].shape
    return pl.pallas_call(
        lambda *refs: downward_kernel(depth, *refs),
        out_shape=jax.ShapeDtypeStruct((up_transfer.shape[0], rank, rhs), f32),
        in_specs=[scalars()] + [whole()] * (depth + 4),
        out_specs=whole(),
        scratch_shapes=[pltpu.VMEM((root_transfer.shape[0], rank, rhs), f32)],
        compiler_params=params(16),
        cost_estimate=cost(1000, 1000),
        name="downward",
    )(local_parent, *siblings, transfer, coupling, root_transfer, up_transfer)


def weights_kernel(count, coupling, out):
    group, slots, _, rank = coupling.shape
    for one in range(group):
        used = count[pl.program_id(0) * group + one]
        for pair in range(slots // 2):
            left = jnp.where(2 * pair < used, coupling[one, 2 * pair], 0.0)
            right = jnp.where(2 * pair + 1 < used, coupling[one, 2 * pair + 1], 0.0)
            both = jnp.concatenate([left, right], axis=1).astype(bf16)
            out[one, :, 2 * pair * rank : 2 * (pair + 1) * rank] = both


def weights(far_count, far_coupling):
    leaves, slots, rank, _ = far_coupling.shape
    group = 4
    return pl.pallas_call(
        weights_kernel,
        out_shape=jax.ShapeDtypeStruct((leaves, rank, slots * rank), bf16),
        grid_spec=pltpu.PrefetchScalarGridSpec(
            num_scalar_prefetch=1,
            grid=(leaves // group,),
            in_specs=[pl.BlockSpec((group, slots, rank, rank), lambda i, n: (i, 0, 0, 0))],
            out_specs=pl.BlockSpec((group, rank, slots * rank), lambda i, n: (i, 0, 0)),
        ),
        compiler_params=params(8, ("arbitrary",)),
        cost_estimate=cost(1000, 1000),
        name="weights",
    )(far_count, in_hbm(far_coupling))


def near_kernel(position, blocks, *refs):
    pieces = refs[:-5]
    out, held, matrices, piece_sems, block_sems = refs[-5:]
    leaves, slots = blocks.shape[:2]
    copies = []
    first = 0
    for index, piece in enumerate(pieces):
        rows = pl.ds(first, piece.shape[0])
        copies.append(pltpu.make_async_copy(piece, held.at[rows], piece_sems.at[index]))
        first += piece.shape[0]
    fetches = [
        pltpu.make_async_copy(blocks.at[leaf], matrices.at[leaf], block_sems.at[leaf]) for leaf in range(leaves)
    ]
    for copy in copies:
        copy.start()
    for fetch in fetches:
        fetch.start()
    for copy in copies:
        copy.wait()
    for leaf in range(leaves):
        fetches[leaf].wait()
        wide = jnp.concatenate([matrices[leaf, slot] for slot in range(slots)], axis=1)
        tall = jnp.concatenate([held[position[leaf * slots + slot]] for slot in range(slots)], axis=0)
        out[leaf] = dot(wide, tall)


def near(position, near_blocks, pieces):
    leaves, slots, size, _ = near_blocks.shape
    rhs = pieces[0].shape[2]
    return pl.pallas_call(
        near_kernel,
        out_shape=jax.ShapeDtypeStruct((leaves, size, rhs), f32),
        in_specs=[scalars()] + [anywhere()] * (1 + len(pieces)),
        out_specs=whole(),
        scratch_shapes=[
            pltpu.VMEM((sum(piece.shape[0] for piece in pieces), size, rhs), bf16),
            pltpu.VMEM(near_blocks.shape, bf16),
            pltpu.SemaphoreType.DMA((len(pieces),)),
            pltpu.SemaphoreType.DMA((leaves,)),
        ],
        compiler_params=params(36),
        cost_estimate=cost(1000, 1000),
        name="near",
    )(position, in_hbm(near_blocks), *[in_hbm(piece) for piece in pieces])


def final_kernel(rows, packed, coefs, on_leaf, bases, near_part, out, *scratch):
    held, picked, results, term, basis, close, load_sems, near_sems, out_sems = scratch
    leaves, rank, wide = packed.shape
    slots = wide // rank
    loads = [
        pltpu.make_async_copy(source, target, load_sems.at[index])
        for index, (source, target) in enumerate(((coefs, held), (on_leaf, term), (bases, basis)))
    ]
    nears = [pltpu.make_async_copy(near_part.at[leaf], close.at[leaf], near_sems.at[leaf]) for leaf in range(leaves)]
    for load in loads + nears:
        load.start()
    for load in loads:
        load.wait()
    stores = []
    for leaf in range(leaves):
        for slot in range(slots):
            picked[leaf, slot * rank : (slot + 1) * rank] = held[rows[leaf * slots + slot]]
        expansion = (term[leaf] + dot(packed[leaf], picked[leaf])).astype(bf16)
        nears[leaf].wait()
        results[leaf] = (dot_t(basis[leaf], expansion) + close[leaf]).astype(bf16)
        stores.append(pltpu.make_async_copy(results.at[leaf], out.at[leaf], out_sems.at[leaf]))
        stores[leaf].start()
    for store in stores:
        store.wait()


def final(far_rows, packed, slab_coefs, on_leaf, bases, near_part):
    leaves, rank, size = bases.shape
    rhs = near_part.shape[2]
    wide = packed.shape[2]
    return pl.pallas_call(
        final_kernel,
        out_shape=jax.ShapeDtypeStruct((leaves, size, rhs), bf16),
        in_specs=[scalars(), whole()] + [anywhere()] * 4,
        out_specs=anywhere(),
        scratch_shapes=[
            pltpu.VMEM(slab_coefs.shape, bf16),
            pltpu.VMEM((leaves, wide, rhs), bf16),
            pltpu.VMEM((leaves, size, rhs), bf16),
            pltpu.VMEM(on_leaf.shape, f32),
            pltpu.VMEM(bases.shape, bf16),
            pltpu.VMEM(near_part.shape, f32),
            pltpu.SemaphoreType.DMA((3,)),
            pltpu.SemaphoreType.DMA((leaves,)),
            pltpu.SemaphoreType.DMA((leaves,)),
        ],
        compiler_params=params(24),
        cost_estimate=cost(1000, 1000),
        name="final",
    )(far_rows, packed, *[in_hbm(array) for array in (slab_coefs, on_leaf, bases, near_part)])


def shifted(array, axis, step, closed):
    count = lax.axis_size(axis)
    pairs = [(i, (i + step) % count) for i in range(count) if closed or 0 <= i + step < count]
    return lax.ppermute(array, axis, pairs)


def both(array, axis, closed):
    return shifted(array, axis, 1, closed), shifted(array, axis, -1, closed)


def after(*arrays):
    return lax.optimization_barrier(arrays)


def partner(array, axis, stride):
    return lax.ppermute(array, axis, [(i, i ^ 1 << stride) for i in range(lax.axis_size(axis))])


def local(
    sources,
    bases,
    leaf_parent,
    up_transfer,
    root_transfer,
    top_transfer,
    top_coupling,
    near_list,
    near_blocks,
    far_list,
    far_count,
    far_coupling,
):
    leaf_total, leaf_size, _ = bases.shape
    bases = bases.transpose(0, 2, 1)
    rhs_count = sources.shape[1]
    cluster_total = leaf_total // 2
    slab_count = lax.axis_size("slab")
    sector_count = lax.axis_size("sector")
    devices = slab_count * sector_count
    depth = devices.bit_length() - 1
    slab_pos = lax.axis_index("slab")
    sector_pos = lax.axis_index("sector")
    device = slab_pos * sector_count + sector_pos
    panels = sources.reshape(leaf_total, leaf_size, rhs_count)

    half = leaf_total // 2
    below, above = both(panels, "slab", False)
    first_sides = both(panels[:half], "sector", True)

    local_parent = leaf_parent - device * cluster_total
    leaf_coefs = leaf_coefficients(panels, bases)
    slab_coefs = lax.all_gather(leaf_coefs, "sector", axis=0, tiled=True)
    current = upward(local_parent, leaf_coefs, up_transfer, root_transfer)
    slots = jnp.arange(2 * depth + 2, dtype=jnp.int32)
    nodes = ((devices + device) >> (slots % depth)) ^ (slots // depth)
    transfer, coupling = tables(nodes[:, None], top_transfer, top_coupling)

    siblings = []

    def climb(level, current):
        siblings.append(partner(current, ("slab", "sector"), level))
        return combine(level, depth + level, current, siblings[-1], transfer)

    current = climb(0, current)
    current, below, above, *first_sides = after(current, below, above, *first_sides)
    first_pair = jnp.concatenate(first_sides)
    first_far = both(first_pair, "slab", False)
    current = climb(1, current)
    second, current = after(panels[half:], current)
    second_sides = both(second, "sector", True)
    current = climb(2, current)
    current, *first_far = after(current, *first_far)
    current = climb(3, current)
    current = climb(4, current)
    current, *second_sides = after(current, *second_sides)
    second_pair = jnp.concatenate(second_sides)
    second_far = both(second_pair, "slab", False)
    current = climb(5, current)
    current, *second_far = after(current, *second_far)
    siblings.append(partner(current, ("slab", "sector"), 6))
    on_leaf = downward(local_parent, siblings, transfer, coupling, root_transfer, up_transfer)

    packed = weights(far_count, far_coupling)

    owner_device = near_list // leaf_total
    slab_offset = (owner_device // sector_count - slab_pos) % 3
    sector_offset = (owner_device % sector_count - sector_pos) % sector_count
    leaf = near_list % leaf_total
    place = leaf // half * (3 * leaf_total) + slab_offset * leaf_total + leaf % half
    place = place + jnp.where(sector_offset == 1, half, 0)
    position = jnp.where(sector_offset == 0, slab_offset * leaf_total + leaf, 3 * leaf_total + place)
    pieces = [panels, above, below]
    for pair, far in ((first_pair, first_far), (second_pair, second_far)):
        pieces += [pair, far[1], far[0]]
    near_part = near(position.reshape(-1), near_blocks, pieces)

    far_rows = (far_list - slab_pos * (sector_count * leaf_total)).reshape(-1)
    field = final(far_rows, packed, slab_coefs, on_leaf, bases, near_part)
    return field.reshape(leaf_total * leaf_size, rhs_count)


def solution(mesh):
    placed = (
        P(("slab", "sector"), None),
        P(("slab", "sector"), None, None),
        P(("slab", "sector")),
        P(("slab", "sector"), None, None),
        P(("slab", "sector"), None, None),
        P(),
        P(),
        P(("slab", "sector"), None),
        P(("slab", "sector"), None, None, None),
        P(("slab", "sector"), None),
        P(("slab", "sector")),
        P(("slab", "sector"), None, None, None),
    )
    return jax.shard_map(
        local, mesh=mesh, in_specs=placed, out_specs=P(("slab", "sector"), None), check_vma=False
    )
```

```python
import jax
import jax.numpy as jnp
from jax import lax
from jax.experimental import pallas as pl
from jax.experimental.pallas import tpu as pltpu
from jax.sharding import PartitionSpec as P

highest = lax.Precision.HIGHEST
f32 = jnp.float32
bf16 = jnp.bfloat16


def dot_t(a, b, precision=None):
    return lax.dot_general(a, b, (((0,), (0,)), ((), ())), precision=precision, preferred_element_type=f32)


def dot(a, b, precision=None):
    return lax.dot_general(a, b, (((1,), (0,)), ((), ())), precision=precision, preferred_element_type=f32)


def dot_r(a, b):
    return lax.dot_general(a, b, (((1,), (1,)), ((), ())), preferred_element_type=f32)


def in_hbm(array):
    return pltpu.with_memory_space_constraint(array, pltpu.HBM)


def whole():
    return pl.BlockSpec(memory_space=pltpu.VMEM)


def anywhere():
    return pl.BlockSpec(memory_space=pl.ANY)


def scalars():
    return pl.BlockSpec(memory_space=pltpu.SMEM)


def params(mib, semantics=None):
    return pltpu.CompilerParams(vmem_limit_bytes=mib << 20, dimension_semantics=semantics)


def cost(flops, nbytes):
    return pl.CostEstimate(flops=flops, bytes_accessed=nbytes, transcendentals=0)


def coefs_kernel(sources, bases, leaf_out, exact_out, held, basis, sems):
    group = sems.shape[0]
    step = held.shape[0] // group
    copies = []
    for part in range(group):
        rows = pl.ds(part * step, step)
        copies.append(
            (
                pltpu.make_async_copy(sources.at[rows], held.at[rows], sems.at[part, 0]),
                pltpu.make_async_copy(bases.at[rows], basis.at[rows], sems.at[part, 1]),
            )
        )
    for pair in copies:
        for copy in pair:
            copy.start()
    for part, pair in enumerate(copies):
        for copy in pair:
            copy.wait()
        for leaf in range(part * step, (part + 1) * step):
            coefs = dot(basis[leaf], held[leaf])
            leaf_out[leaf] = coefs.astype(bf16)
            exact_out[leaf] = coefs


def leaf_coefficients(panels, bases):
    leaves, size, rhs = panels.shape
    rank = bases.shape[1]
    return pl.pallas_call(
        coefs_kernel,
        out_shape=(
            jax.ShapeDtypeStruct((leaves, rank, rhs), bf16),
            jax.ShapeDtypeStruct((leaves, rank, rhs), f32),
        ),
        in_specs=[anywhere(), anywhere()],
        out_specs=(whole(), whole()),
        scratch_shapes=[
            pltpu.VMEM((leaves, size, rhs), bf16),
            pltpu.VMEM((leaves, rank, size), bf16),
            pltpu.SemaphoreType.DMA((4, 2)),
        ],
        compiler_params=params(8),
        cost_estimate=cost(1000, 1000),
        name="coefs",
    )(in_hbm(panels), in_hbm(bases))


def upward_kernel(parent, coefs, up, root, root_out, clusters):
    clusters[...] = jnp.zeros_like(clusters)
    for leaf in range(coefs.shape[0]):
        clusters[parent[leaf]] += dot_t(up[leaf], coefs[leaf], highest)
    total = dot_t(root[0], clusters[0], highest)
    for cluster in range(1, root.shape[0]):
        total = total + dot_t(root[cluster], clusters[cluster], highest)
    root_out[...] = total


def upward(local_parent, leaf_coefs, up_transfer, root_transfer):
    leaves, rank, rhs = leaf_coefs.shape
    return pl.pallas_call(
        upward_kernel,
        out_shape=jax.ShapeDtypeStruct((rank, rhs), f32),
        in_specs=[scalars(), whole(), whole(), whole()],
        out_specs=whole(),
        scratch_shapes=[pltpu.VMEM((root_transfer.shape[0], rank, rhs), f32)],
        compiler_params=params(8),
        cost_estimate=cost(1000, 1000),
        name="upward",
    )(local_parent, leaf_coefs, up_transfer, root_transfer)


def tables_kernel(nodes, transfer, coupling, transfer_out, coupling_out, held, sems):
    parts = sems.shape[1]
    step = held.shape[1] // parts
    rank, size = held.shape[2:]
    ids = lax.broadcasted_iota(jnp.int32, (nodes.shape[0], size), 1)
    chosen = (ids == nodes[...]).astype(bf16)
    copies = []
    for kind, table in enumerate((transfer, coupling)):
        for part in range(parts):
            rows = pl.ds(part * step, step)
            copies.append(pltpu.make_async_copy(table.at[rows], held.at[kind, rows], sems.at[kind, part]))
    for copy in copies:
        copy.start()
    for kind, out in enumerate((transfer_out, coupling_out)):
        for part in range(parts):
            copies[kind * parts + part].wait()
            first = part * step
            values = held[kind, first : first + step].reshape(-1, size)
            high = values.astype(bf16)
            low = (values - high.astype(f32)).astype(bf16)
            rows = dot_r(chosen, high) + dot_r(chosen, low)
            for row in range(step):
                out[:, first + row, :] = rows[:, row * rank : (row + 1) * rank]


def tables(nodes, transfer, coupling):
    count = nodes.shape[0]
    size, rank, _ = transfer.shape
    return pl.pallas_call(
        tables_kernel,
        out_shape=(jax.ShapeDtypeStruct((count, rank, rank), f32),) * 2,
        in_specs=[whole(), anywhere(), anywhere()],
        out_specs=(whole(),) * 2,
        scratch_shapes=[pltpu.VMEM((2, rank, rank, size), f32), pltpu.SemaphoreType.DMA((2, 8))],
        compiler_params=params(20),
        cost_estimate=cost(1000, 1000),
        name="tables",
    )(nodes, in_hbm(transfer.transpose(1, 2, 0)), in_hbm(coupling.transpose(1, 2, 0)))


def combine_kernel(own, other, current, sibling, mats, out):
    total = dot_t(mats[own], current[...], highest)
    out[...] = total + dot_t(mats[other], sibling[...], highest)


def combine(own, other, current, sibling, mats):
    return pl.pallas_call(
        lambda *refs: combine_kernel(own, other, *refs),
        out_shape=jax.ShapeDtypeStruct(current.shape, f32),
        in_specs=[whole(), whole(), whole()],
        out_specs=whole(),
        compiler_params=params(4),
        cost_estimate=cost(1000, 1000),
        name="combine",
    )(current, sibling, mats)


def combine_four_kernel(picks, root, one, two, three, mats, sibling_out, out):
    own, other, second, third, own_up, other_up = picks
    sibling = dot_t(mats[second], two[...], highest) + dot_t(mats[third], three[...], highest)
    sibling_out[...] = sibling
    lower = dot_t(mats[own], root[...], highest) + dot_t(mats[other], one[...], highest)
    out[...] = dot_t(mats[own_up], lower, highest) + dot_t(mats[other_up], sibling, highest)


def combine_four(picks, roots, mats):
    return pl.pallas_call(
        lambda *refs: combine_four_kernel(picks, *refs),
        out_shape=(jax.ShapeDtypeStruct(roots[0].shape, f32),) * 2,
        in_specs=[whole()] * 5,
        out_specs=(whole(),) * 2,
        compiler_params=params(2),
        cost_estimate=cost(1000, 1000),
        name="combine_four",
    )(*roots, mats)


def downward_kernel(depth, parent, *refs):
    siblings = refs[:depth]
    transfer, coupling, root, up, out, clusters = refs[depth:]
    down = dot(coupling[depth - 1], siblings[depth - 1][...], highest)
    for level in reversed(range(depth - 1)):
        across = dot(coupling[level], siblings[level][...], highest)
        down = across + dot(transfer[level], down, highest)
    for cluster in range(root.shape[0]):
        clusters[cluster] = dot(root[cluster], down, highest)
    for leaf in range(up.shape[0]):
        out[leaf] = dot(up[leaf], clusters[parent[leaf]], highest)


def downward(local_parent, siblings, transfer, coupling, root_transfer, up_transfer):
    depth = len(siblings)
    rank, rhs = siblings[0].shape
    return pl.pallas_call(
        lambda *refs: downward_kernel(depth, *refs),
        out_shape=jax.ShapeDtypeStruct((up_transfer.shape[0], rank, rhs), f32),
        in_specs=[scalars()] + [whole()] * (depth + 4),
        out_specs=whole(),
        scratch_shapes=[pltpu.VMEM((root_transfer.shape[0], rank, rhs), f32)],
        compiler_params=params(16),
        cost_estimate=cost(1000, 1000),
        name="downward",
    )(local_parent, *siblings, transfer, coupling, root_transfer, up_transfer)


def weights_kernel(count, coupling, out, held, sems):
    leaves, slots, _, rank = coupling.shape
    copies = [pltpu.make_async_copy(coupling.at[leaf], held.at[leaf], sems.at[leaf]) for leaf in range(leaves)]
    for copy in copies:
        copy.start()
    for leaf in range(leaves):
        used = count[leaf]
        copies[leaf].wait()
        for pair in range(slots // 2):
            left = jnp.where(2 * pair < used, held[leaf, 2 * pair], 0.0)
            right = jnp.where(2 * pair + 1 < used, held[leaf, 2 * pair + 1], 0.0)
            joined = jnp.concatenate([left, right], axis=1).astype(bf16)
            out[leaf, :, 2 * pair * rank : 2 * (pair + 1) * rank] = joined


def weights(far_count, far_coupling):
    leaves, slots, rank, _ = far_coupling.shape
    return pl.pallas_call(
        weights_kernel,
        out_shape=jax.ShapeDtypeStruct((leaves, rank, slots * rank), bf16),
        in_specs=[scalars(), anywhere()],
        out_specs=whole(),
        scratch_shapes=[pltpu.VMEM(far_coupling.shape, f32), pltpu.SemaphoreType.DMA((leaves,))],
        compiler_params=params(20),
        cost_estimate=cost(1000, 1000),
        name="weights",
    )(far_count, in_hbm(far_coupling))


def near_kernel(position, blocks, *refs):
    pieces = refs[:-5]
    out, held, matrices, piece_sems, block_sems = refs[-5:]
    leaves, slots = blocks.shape[:2]
    copies = []
    first = 0
    for index, piece in enumerate(pieces):
        rows = pl.ds(first, piece.shape[0])
        copies.append(pltpu.make_async_copy(piece, held.at[rows], piece_sems.at[index]))
        first += piece.shape[0]
    fetches = [
        pltpu.make_async_copy(blocks.at[leaf], matrices.at[leaf], block_sems.at[leaf]) for leaf in range(leaves)
    ]
    for copy in copies:
        copy.start()
    for fetch in fetches:
        fetch.start()
    for copy in copies:
        copy.wait()
    for leaf in range(leaves):
        fetches[leaf].wait()
        wide = jnp.concatenate([matrices[leaf, slot] for slot in range(slots)], axis=1)
        tall = jnp.concatenate([held[position[leaf * slots + slot]] for slot in range(slots)], axis=0)
        out[leaf] = dot(wide, tall)


def near(position, near_blocks, pieces):
    leaves, slots, size, _ = near_blocks.shape
    rhs = pieces[0].shape[2]
    return pl.pallas_call(
        near_kernel,
        out_shape=jax.ShapeDtypeStruct((leaves, size, rhs), f32),
        in_specs=[scalars()] + [anywhere()] * (1 + len(pieces)),
        out_specs=whole(),
        scratch_shapes=[
            pltpu.VMEM((sum(piece.shape[0] for piece in pieces), size, rhs), bf16),
            pltpu.VMEM(near_blocks.shape, bf16),
            pltpu.SemaphoreType.DMA((len(pieces),)),
            pltpu.SemaphoreType.DMA((leaves,)),
        ],
        compiler_params=params(36),
        cost_estimate=cost(1000, 1000),
        name="near",
    )(position, in_hbm(near_blocks), *[in_hbm(piece) for piece in pieces])


def final_kernel(rows, packed, coefs, on_leaf, bases, near_part, out, *scratch):
    held, picked, results, term, basis, close, load_sems, near_sems, out_sems = scratch
    leaves, rank, wide = packed.shape
    slots = wide // rank
    loads = [
        pltpu.make_async_copy(source, target, load_sems.at[index])
        for index, (source, target) in enumerate(((coefs, held), (on_leaf, term), (bases, basis)))
    ]
    nears = [pltpu.make_async_copy(near_part.at[leaf], close.at[leaf], near_sems.at[leaf]) for leaf in range(leaves)]
    for load in loads + nears:
        load.start()
    for load in loads:
        load.wait()
    stores = []
    for leaf in range(leaves):
        for slot in range(slots):
            picked[leaf, slot * rank : (slot + 1) * rank] = held[rows[leaf * slots + slot]]
        expansion = (term[leaf] + dot(packed[leaf], picked[leaf])).astype(bf16)
        nears[leaf].wait()
        results[leaf] = (dot_t(basis[leaf], expansion) + close[leaf]).astype(bf16)
        stores.append(pltpu.make_async_copy(results.at[leaf], out.at[leaf], out_sems.at[leaf]))
        stores[leaf].start()
    for store in stores:
        store.wait()


def final(far_rows, packed, slab_coefs, on_leaf, bases, near_part):
    leaves, rank, size = bases.shape
    rhs = near_part.shape[2]
    wide = packed.shape[2]
    return pl.pallas_call(
        final_kernel,
        out_shape=jax.ShapeDtypeStruct((leaves, size, rhs), bf16),
        in_specs=[scalars(), whole()] + [anywhere()] * 4,
        out_specs=anywhere(),
        scratch_shapes=[
            pltpu.VMEM(slab_coefs.shape, bf16),
            pltpu.VMEM((leaves, wide, rhs), bf16),
            pltpu.VMEM((leaves, size, rhs), bf16),
            pltpu.VMEM(on_leaf.shape, f32),
            pltpu.VMEM(bases.shape, bf16),
            pltpu.VMEM(near_part.shape, f32),
            pltpu.SemaphoreType.DMA((3,)),
            pltpu.SemaphoreType.DMA((leaves,)),
            pltpu.SemaphoreType.DMA((leaves,)),
        ],
        compiler_params=params(24),
        cost_estimate=cost(1000, 1000),
        name="final",
    )(far_rows, packed, *[in_hbm(array) for array in (slab_coefs, on_leaf, bases, near_part)])


def shifted(array, axis, step, closed):
    count = lax.axis_size(axis)
    pairs = [(i, (i + step) % count) for i in range(count) if closed or 0 <= i + step < count]
    return lax.ppermute(array, axis, pairs)


def both(array, axis, closed):
    return shifted(array, axis, 1, closed), shifted(array, axis, -1, closed)


def after(*arrays):
    return lax.optimization_barrier(arrays)


def partner(array, axis, flip):
    return lax.ppermute(array, axis, [(i, i ^ flip) for i in range(lax.axis_size(axis))])


def local(
    sources,
    bases,
    leaf_parent,
    up_transfer,
    root_transfer,
    top_transfer,
    top_coupling,
    near_list,
    near_blocks,
    far_list,
    far_count,
    far_coupling,
):
    leaf_total, leaf_size, _ = bases.shape
    bases = bases.transpose(0, 2, 1)
    rhs_count = sources.shape[1]
    cluster_total = leaf_total // 2
    slab_count = lax.axis_size("slab")
    sector_count = lax.axis_size("sector")
    devices = slab_count * sector_count
    depth = devices.bit_length() - 1
    slab_pos = lax.axis_index("slab")
    sector_pos = lax.axis_index("sector")
    device = slab_pos * sector_count + sector_pos
    panels = sources.reshape(leaf_total, leaf_size, rhs_count)

    sides = both(panels, "sector", True)
    below, above = both(panels, "slab", False)
    local_parent = leaf_parent - device * cluster_total
    leaf_coefs, exact_coefs = leaf_coefficients(panels, bases)
    slab_coefs = lax.all_gather(leaf_coefs, "sector", axis=0, tiled=True)
    root = upward(local_parent, exact_coefs, up_transfer, root_transfer)
    slots = jnp.arange(24, dtype=jnp.int32)
    starts = [0, 2, 5]
    level_of = jnp.where(slots < 2 * depth, slots % depth, (slots - 2 * depth) // 2 * 5 // 2)
    flips = jnp.where(slots < 2 * depth, slots // depth, 2 + slots % 2)
    nodes = ((devices + device) >> jnp.minimum(level_of, depth - 1)) ^ flips
    transfer, coupling = tables(nodes[:, None], top_transfer, top_coupling)
    both_axes = ("slab", "sector")

    def exchange(level, root):
        return [root] + [partner(root, both_axes, flip << level) for flip in (1, 2, 3)]

    def climb(level, quad):
        extra = 2 * depth + 2 * starts.index(level)
        picks = (level, depth + level, extra, extra + 1, level + 1, depth + level + 1)
        return combine_four(picks, quad, transfer)

    packed = weights(far_count, far_coupling)
    root, below, above, transfer, packed = after(root, below, above, transfer, packed)
    quad = exchange(0, root)
    quad[0], *sides = after(quad[0], *sides)
    pair = jnp.concatenate(sides)
    far = both(pair, "slab", False)
    across, current = climb(0, quad)
    siblings = [quad[1], across]
    quad = exchange(2, current)
    across, current = climb(2, quad)
    siblings += [quad[1], across]
    siblings.append(partner(current, both_axes, 1 << 4))
    current = combine(4, depth + 4, current, siblings[-1], transfer)
    current, *far = after(current, *far)
    quad = exchange(5, current)
    across, _ = climb(5, quad)
    siblings += [quad[1], across]
    on_leaf = downward(local_parent, siblings, transfer, coupling, root_transfer, up_transfer)

    owner_device = near_list // leaf_total
    slab_offset = (owner_device // sector_count - slab_pos) % 3
    sector_offset = (owner_device % sector_count - sector_pos) % sector_count
    side = (3 + 2 * slab_offset + jnp.where(sector_offset == 1, 1, 0)) * leaf_total
    position = jnp.where(sector_offset == 0, slab_offset * leaf_total, side) + near_list % leaf_total
    pieces = [panels, above, below, pair, far[1], far[0]]
    near_part = near(position.reshape(-1), near_blocks, pieces)

    far_rows = (far_list - slab_pos * (sector_count * leaf_total)).reshape(-1)
    field = final(far_rows, packed, slab_coefs, on_leaf, bases, near_part)
    return field.reshape(leaf_total * leaf_size, rhs_count)


def solution(mesh):
    placed = (
        P(("slab", "sector"), None),
        P(("slab", "sector"), None, None),
        P(("slab", "sector")),
        P(("slab", "sector"), None, None),
        P(("slab", "sector"), None, None),
        P(),
        P(),
        P(("slab", "sector"), None),
        P(("slab", "sector"), None, None, None),
        P(("slab", "sector"), None),
        P(("slab", "sector")),
        P(("slab", "sector"), None, None, None),
    )
    return jax.shard_map(
        local, mesh=mesh, in_specs=placed, out_specs=P(("slab", "sector"), None), check_vma=False
    )
```

```python
import jax
import jax.numpy as jnp
from jax import lax
from jax.experimental import pallas as pl
from jax.experimental.pallas import tpu as pltpu
from jax.sharding import PartitionSpec as P

highest = lax.Precision.HIGHEST
f32 = jnp.float32
bf16 = jnp.bfloat16


def dot_t(a, b, precision=None):
    return lax.dot_general(a, b, (((0,), (0,)), ((), ())), precision=precision, preferred_element_type=f32)


def dot(a, b, precision=None):
    return lax.dot_general(a, b, (((1,), (0,)), ((), ())), precision=precision, preferred_element_type=f32)


def dot_r(a, b):
    return lax.dot_general(a, b, (((1,), (1,)), ((), ())), preferred_element_type=f32)


def in_hbm(array):
    return pltpu.with_memory_space_constraint(array, pltpu.HBM)


def whole():
    return pl.BlockSpec(memory_space=pltpu.VMEM)


def anywhere():
    return pl.BlockSpec(memory_space=pl.ANY)


def scalars():
    return pl.BlockSpec(memory_space=pltpu.SMEM)


def params(mib, semantics=None):
    return pltpu.CompilerParams(vmem_limit_bytes=mib << 20, dimension_semantics=semantics)


def cost(flops, nbytes):
    return pl.CostEstimate(flops=flops, bytes_accessed=nbytes, transcendentals=0)


def coefs_kernel(parent, sources, bases, up, root, leaf_out, root_out, held, basis, up_held, root_held, clusters, sems, tail_sems):
    group = sems.shape[0]
    step = held.shape[0] // group
    copies = []
    for part in range(group):
        rows = pl.ds(part * step, step)
        copies.append(pltpu.make_async_copy(sources.at[rows], held.at[rows], sems.at[part, 0]))
        copies.append(pltpu.make_async_copy(bases.at[rows], basis.at[rows], sems.at[part, 1]))
    tails = [
        pltpu.make_async_copy(up, up_held, tail_sems.at[0]),
        pltpu.make_async_copy(root, root_held, tail_sems.at[1]),
    ]
    for copy in copies + tails:
        copy.start()
    clusters[...] = jnp.zeros_like(clusters)
    exact = []
    for part in range(group):
        copies[2 * part].wait()
        copies[2 * part + 1].wait()
        for leaf in range(part * step, (part + 1) * step):
            exact.append(dot(basis[leaf], held[leaf]))
            leaf_out[leaf] = exact[leaf].astype(bf16)
    for tail in tails:
        tail.wait()
    for leaf, coefs in enumerate(exact):
        clusters[parent[leaf]] += dot_t(up_held[leaf], coefs, highest)
    total = dot_t(root_held[0], clusters[0], highest)
    for cluster in range(1, root_held.shape[0]):
        total = total + dot_t(root_held[cluster], clusters[cluster], highest)
    root_out[...] = total


def leaf_coefficients(local_parent, panels, bases, up_transfer, root_transfer):
    leaves, size, rhs = panels.shape
    rank = bases.shape[1]
    return pl.pallas_call(
        coefs_kernel,
        out_shape=(
            jax.ShapeDtypeStruct((leaves, rank, rhs), bf16),
            jax.ShapeDtypeStruct((rank, rhs), f32),
        ),
        in_specs=[scalars()] + [anywhere()] * 4,
        out_specs=(whole(), whole()),
        scratch_shapes=[
            pltpu.VMEM((leaves, size, rhs), bf16),
            pltpu.VMEM((leaves, rank, size), bf16),
            pltpu.VMEM(up_transfer.shape, f32),
            pltpu.VMEM(root_transfer.shape, f32),
            pltpu.VMEM((root_transfer.shape[0], rank, rhs), f32),
            pltpu.SemaphoreType.DMA((4, 2)),
            pltpu.SemaphoreType.DMA((2,)),
        ],
        compiler_params=params(12),
        cost_estimate=cost(1000, 1000),
        name="coefs",
    )(local_parent, *[in_hbm(array) for array in (panels, bases, up_transfer, root_transfer)])


def tables_kernel(nodes, transfer, coupling, transfer_out, coupling_out, held, sems):
    parts = sems.shape[1]
    step = held.shape[1] // parts
    rank, size = held.shape[2:]
    ids = lax.broadcasted_iota(jnp.int32, (nodes.shape[0], size), 1)
    chosen = (ids == nodes[...]).astype(bf16)
    copies = []
    for kind, table in enumerate((transfer, coupling)):
        for part in range(parts):
            rows = pl.ds(part * step, step)
            copies.append(pltpu.make_async_copy(table.at[rows], held.at[kind, rows], sems.at[kind, part]))
    for copy in copies:
        copy.start()
    for kind, out in enumerate((transfer_out, coupling_out)):
        for part in range(parts):
            copies[kind * parts + part].wait()
            first = part * step
            values = held[kind, first : first + step].reshape(-1, size)
            high = values.astype(bf16)
            low = (values - high.astype(f32)).astype(bf16)
            rows = dot_r(chosen, high) + dot_r(chosen, low)
            for row in range(step):
                out[:, first + row, :] = rows[:, row * rank : (row + 1) * rank]


def tables(nodes, transfer, coupling):
    count = nodes.shape[0]
    size, rank, _ = transfer.shape
    return pl.pallas_call(
        tables_kernel,
        out_shape=(jax.ShapeDtypeStruct((count, rank, rank), f32),) * 2,
        in_specs=[whole(), anywhere(), anywhere()],
        out_specs=(whole(),) * 2,
        scratch_shapes=[pltpu.VMEM((2, rank, rank, size), f32), pltpu.SemaphoreType.DMA((2, 8))],
        compiler_params=params(20),
        cost_estimate=cost(1000, 1000),
        name="tables",
    )(nodes, in_hbm(transfer.transpose(1, 2, 0)), in_hbm(coupling.transpose(1, 2, 0)))


def combine_kernel(own, other, current, sibling, mats, out):
    total = dot_t(mats[own], current[...], highest)
    out[...] = total + dot_t(mats[other], sibling[...], highest)


def combine(own, other, current, sibling, mats):
    return pl.pallas_call(
        lambda *refs: combine_kernel(own, other, *refs),
        out_shape=jax.ShapeDtypeStruct(current.shape, f32),
        in_specs=[whole(), whole(), whole()],
        out_specs=whole(),
        compiler_params=params(4),
        cost_estimate=cost(1000, 1000),
        name="combine",
    )(current, sibling, mats)


def combine_four_kernel(picks, root, one, two, three, mats, sibling_out, out):
    own, other, second, third, own_up, other_up = picks
    sibling = dot_t(mats[second], two[...], highest) + dot_t(mats[third], three[...], highest)
    sibling_out[...] = sibling
    lower = dot_t(mats[own], root[...], highest) + dot_t(mats[other], one[...], highest)
    out[...] = dot_t(mats[own_up], lower, highest) + dot_t(mats[other_up], sibling, highest)


def combine_four(picks, roots, mats):
    return pl.pallas_call(
        lambda *refs: combine_four_kernel(picks, *refs),
        out_shape=(jax.ShapeDtypeStruct(roots[0].shape, f32),) * 2,
        in_specs=[whole()] * 5,
        out_specs=(whole(),) * 2,
        compiler_params=params(2),
        cost_estimate=cost(1000, 1000),
        name="combine_four",
    )(*roots, mats)


def downward_kernel(depth, parent, *refs):
    siblings = refs[:depth]
    transfer, coupling, root, up, out, clusters = refs[depth:]
    down = dot(coupling[depth - 1], siblings[depth - 1][...], highest)
    for level in reversed(range(depth - 1)):
        across = dot(coupling[level], siblings[level][...], highest)
        down = across + dot(transfer[level], down, highest)
    for cluster in range(root.shape[0]):
        clusters[cluster] = dot(root[cluster], down, highest)
    for leaf in range(up.shape[0]):
        out[leaf] = dot(up[leaf], clusters[parent[leaf]], highest)


def downward(local_parent, siblings, transfer, coupling, root_transfer, up_transfer):
    depth = len(siblings)
    rank, rhs = siblings[0].shape
    return pl.pallas_call(
        lambda *refs: downward_kernel(depth, *refs),
        out_shape=jax.ShapeDtypeStruct((up_transfer.shape[0], rank, rhs), f32),
        in_specs=[scalars()] + [whole()] * (depth + 4),
        out_specs=whole(),
        scratch_shapes=[pltpu.VMEM((root_transfer.shape[0], rank, rhs), f32)],
        compiler_params=params(16),
        cost_estimate=cost(1000, 1000),
        name="downward",
    )(local_parent, *siblings, transfer, coupling, root_transfer, up_transfer)


def weights_kernel(count, coupling, out, held, sems):
    leaves, slots, _, rank = coupling.shape
    copies = [pltpu.make_async_copy(coupling.at[leaf], held.at[leaf], sems.at[leaf]) for leaf in range(leaves)]
    for copy in copies:
        copy.start()
    for leaf in range(leaves):
        used = count[leaf]
        copies[leaf].wait()
        for pair in range(slots // 2):
            left = jnp.where(2 * pair < used, held[leaf, 2 * pair], 0.0)
            right = jnp.where(2 * pair + 1 < used, held[leaf, 2 * pair + 1], 0.0)
            joined = jnp.concatenate([left, right], axis=1).astype(bf16)
            out[leaf, :, 2 * pair * rank : 2 * (pair + 1) * rank] = joined


def weights(far_count, far_coupling):
    leaves, slots, rank, _ = far_coupling.shape
    return pl.pallas_call(
        weights_kernel,
        out_shape=jax.ShapeDtypeStruct((leaves, rank, slots * rank), bf16),
        in_specs=[scalars(), anywhere()],
        out_specs=whole(),
        scratch_shapes=[pltpu.VMEM(far_coupling.shape, f32), pltpu.SemaphoreType.DMA((leaves,))],
        compiler_params=params(20),
        cost_estimate=cost(1000, 1000),
        name="weights",
    )(far_count, in_hbm(far_coupling))


def near_kernel(position, blocks, *refs):
    pieces = refs[:-5]
    out, held, matrices, piece_sems, block_sems = refs[-5:]
    leaves, slots = blocks.shape[:2]
    copies = []
    first = 0
    for index, piece in enumerate(pieces):
        rows = pl.ds(first, piece.shape[0])
        copies.append(pltpu.make_async_copy(piece, held.at[rows], piece_sems.at[index]))
        first += piece.shape[0]
    fetches = [
        pltpu.make_async_copy(blocks.at[leaf], matrices.at[leaf], block_sems.at[leaf]) for leaf in range(leaves)
    ]
    for copy in copies + fetches[:1]:
        copy.start()
    for copy in copies:
        copy.wait()
    for fetch in fetches[1:]:
        fetch.start()
    for leaf in range(leaves):
        fetches[leaf].wait()
        wide = jnp.concatenate([matrices[leaf, slot] for slot in range(slots)], axis=1)
        tall = jnp.concatenate([held[position[leaf * slots + slot]] for slot in range(slots)], axis=0)
        out[leaf] = dot(wide, tall)


def near(position, near_blocks, pieces):
    leaves, slots, size, _ = near_blocks.shape
    rhs = pieces[0].shape[2]
    return pl.pallas_call(
        near_kernel,
        out_shape=jax.ShapeDtypeStruct((leaves, size, rhs), f32),
        in_specs=[scalars()] + [anywhere()] * (1 + len(pieces)),
        out_specs=whole(),
        scratch_shapes=[
            pltpu.VMEM((sum(piece.shape[0] for piece in pieces), size, rhs), bf16),
            pltpu.VMEM(near_blocks.shape, bf16),
            pltpu.SemaphoreType.DMA((len(pieces),)),
            pltpu.SemaphoreType.DMA((leaves,)),
        ],
        compiler_params=params(36),
        cost_estimate=cost(1000, 1000),
        name="near",
    )(position, in_hbm(near_blocks), *pieces)


def final_kernel(rows, packed, coefs, on_leaf, bases, near_part, out, *scratch):
    held, picked, results, term, basis, close, load_sems, near_sems, out_sems = scratch
    leaves, rank, wide = packed.shape
    slots = wide // rank
    loads = [
        pltpu.make_async_copy(source, target, load_sems.at[index])
        for index, (source, target) in enumerate(((coefs, held), (on_leaf, term), (bases, basis)))
    ]
    nears = [pltpu.make_async_copy(near_part.at[leaf], close.at[leaf], near_sems.at[leaf]) for leaf in range(leaves)]
    for load in loads:
        load.start()
    for load in loads:
        load.wait()
    for load in nears:
        load.start()
    stores = []
    for leaf in range(leaves):
        for slot in range(slots):
            picked[leaf, slot * rank : (slot + 1) * rank] = held[rows[leaf * slots + slot]]
        expansion = (term[leaf] + dot(packed[leaf], picked[leaf])).astype(bf16)
        nears[leaf].wait()
        results[leaf] = (dot_t(basis[leaf], expansion) + close[leaf]).astype(bf16)
        stores.append(pltpu.make_async_copy(results.at[leaf], out.at[leaf], out_sems.at[leaf]))
        stores[leaf].start()
    for store in stores:
        store.wait()


def final(far_rows, packed, slab_coefs, on_leaf, bases, near_part):
    leaves, rank, size = bases.shape
    rhs = near_part.shape[2]
    wide = packed.shape[2]
    return pl.pallas_call(
        final_kernel,
        out_shape=jax.ShapeDtypeStruct((leaves, size, rhs), bf16),
        in_specs=[scalars(), whole()] + [anywhere()] * 4,
        out_specs=anywhere(),
        scratch_shapes=[
            pltpu.VMEM(slab_coefs.shape, bf16),
            pltpu.VMEM((leaves, wide, rhs), bf16),
            pltpu.VMEM((leaves, size, rhs), bf16),
            pltpu.VMEM(on_leaf.shape, f32),
            pltpu.VMEM(bases.shape, bf16),
            pltpu.VMEM(near_part.shape, f32),
            pltpu.SemaphoreType.DMA((3,)),
            pltpu.SemaphoreType.DMA((leaves,)),
            pltpu.SemaphoreType.DMA((leaves,)),
        ],
        compiler_params=params(24),
        cost_estimate=cost(1000, 1000),
        name="final",
    )(far_rows, packed, *[in_hbm(array) for array in (slab_coefs, on_leaf, bases, near_part)])


def shifted(array, axis, step, closed):
    count = lax.axis_size(axis)
    pairs = [(i, (i + step) % count) for i in range(count) if closed or 0 <= i + step < count]
    return lax.ppermute(array, axis, pairs)


def both(array, axis, closed):
    return shifted(array, axis, 1, closed), shifted(array, axis, -1, closed)


def after(*arrays):
    return lax.optimization_barrier(arrays)


def partner(array, axis, flip):
    return lax.ppermute(array, axis, [(i, i ^ flip) for i in range(lax.axis_size(axis))])


def local(
    sources,
    bases,
    leaf_parent,
    up_transfer,
    root_transfer,
    top_transfer,
    top_coupling,
    near_list,
    near_blocks,
    far_list,
    far_count,
    far_coupling,
):
    leaf_total, leaf_size, _ = bases.shape
    bases = bases.transpose(0, 2, 1)
    rhs_count = sources.shape[1]
    cluster_total = leaf_total // 2
    slab_count = lax.axis_size("slab")
    sector_count = lax.axis_size("sector")
    devices = slab_count * sector_count
    depth = devices.bit_length() - 1
    slab_pos = lax.axis_index("slab")
    sector_pos = lax.axis_index("sector")
    device = slab_pos * sector_count + sector_pos
    panels = sources.reshape(leaf_total, leaf_size, rhs_count)

    local_parent = leaf_parent - device * cluster_total
    leaf_coefs, root = leaf_coefficients(local_parent, panels, bases, up_transfer, root_transfer)
    slab_coefs = lax.all_gather(leaf_coefs, "sector", axis=0, tiled=True)

    owner_device = near_list // leaf_total
    slab_offset = (owner_device // sector_count - slab_pos) % 3
    sector_offset = (owner_device % sector_count - sector_pos) % sector_count
    row = jnp.where(sector_offset == 0, 0, jnp.where(sector_offset == 1, 6, 3)) + slab_offset
    position = (row * leaf_total + near_list % leaf_total).reshape(-1)
    far_rows = (far_list - slab_pos * (sector_count * leaf_total)).reshape(-1)

    both_axes = ("slab", "sector")
    quad = [root] + [partner(root, both_axes, flip) for flip in (1, 2, 3)]
    shared, *quad = after(panels, *quad)
    sides = both(shared, "sector", True)
    below, above = both(shared, "slab", False)
    slots = jnp.arange(2 * depth + 2, dtype=jnp.int32)
    level_of = jnp.where(slots < 2 * depth, slots % depth, 0)
    flips = jnp.where(slots < 2 * depth, slots // depth, 2 + slots % 2)
    nodes = ((devices + device) >> level_of) ^ flips
    nodes, position, far_rows, *quad = after(nodes, position, far_rows, *quad)
    transfer, coupling = tables(nodes[:, None], top_transfer, top_coupling)

    picks = (0, depth, 2 * depth, 2 * depth + 1, 1, depth + 1)
    across, current = combine_four(picks, quad, transfer)
    siblings = [quad[1], across]
    for level in range(2, depth):
        if level == depth - 2:
            current, below, above, *sides = after(current, below, above, *sides)
        siblings.append(partner(current, both_axes, 1 << level))
        if level < depth - 1:
            current = combine(level, depth + level, current, siblings[-1], transfer)
    corners = [both(side, "slab", False) for side in sides]
    on_leaf = downward(local_parent, siblings, transfer, coupling, root_transfer, up_transfer)

    packed = weights(far_count, far_coupling)
    pieces = [panels, above, below]
    for side, corner in zip(sides, corners):
        pieces += [side, corner[1], corner[0]]
    near_part = near(position, near_blocks, pieces)

    field = final(far_rows, packed, slab_coefs, on_leaf, bases, near_part)
    return field.reshape(leaf_total * leaf_size, rhs_count)


def solution(mesh):
    placed = (
        P(("slab", "sector"), None),
        P(("slab", "sector"), None, None),
        P(("slab", "sector")),
        P(("slab", "sector"), None, None),
        P(("slab", "sector"), None, None),
        P(),
        P(),
        P(("slab", "sector"), None),
        P(("slab", "sector"), None, None, None),
        P(("slab", "sector"), None),
        P(("slab", "sector")),
        P(("slab", "sector"), None, None, None),
    )
    return jax.shard_map(
        local, mesh=mesh, in_specs=placed, out_specs=P(("slab", "sector"), None), check_vma=False
    )
```

```python
import jax
import jax.numpy as jnp
from jax import lax
from jax.experimental import pallas as pl
from jax.experimental.pallas import tpu as pltpu
from jax.sharding import PartitionSpec as P

highest = lax.Precision.HIGHEST
f32 = jnp.float32
bf16 = jnp.bfloat16


def dot_t(a, b, precision=None):
    return lax.dot_general(a, b, (((0,), (0,)), ((), ())), precision=precision, preferred_element_type=f32)


def dot(a, b, precision=None):
    return lax.dot_general(a, b, (((1,), (0,)), ((), ())), precision=precision, preferred_element_type=f32)


def dot_r(a, b):
    return lax.dot_general(a, b, (((1,), (1,)), ((), ())), preferred_element_type=f32)


def in_hbm(array):
    return pltpu.with_memory_space_constraint(array, pltpu.HBM)


def whole():
    return pl.BlockSpec(memory_space=pltpu.VMEM)


def anywhere():
    return pl.BlockSpec(memory_space=pl.ANY)


def scalars():
    return pl.BlockSpec(memory_space=pltpu.SMEM)


def params(mib, semantics=None):
    return pltpu.CompilerParams(vmem_limit_bytes=mib << 20, dimension_semantics=semantics)


def cost(flops, nbytes):
    return pl.CostEstimate(flops=flops, bytes_accessed=nbytes, transcendentals=0)


def coefs_kernel(parent, sources, bases, up, root, leaf_out, root_out, held, basis, up_held, root_held, clusters, sems, tail_sems):
    group = sems.shape[0]
    step = held.shape[0] // group
    copies = []
    for part in range(group):
        rows = pl.ds(part * step, step)
        copies.append(pltpu.make_async_copy(sources.at[rows], held.at[rows], sems.at[part, 0]))
        copies.append(pltpu.make_async_copy(bases.at[rows], basis.at[rows], sems.at[part, 1]))
    tails = [
        pltpu.make_async_copy(up, up_held, tail_sems.at[0]),
        pltpu.make_async_copy(root, root_held, tail_sems.at[1]),
    ]
    for copy in copies + tails:
        copy.start()
    clusters[...] = jnp.zeros_like(clusters)
    exact = []
    for part in range(group):
        copies[2 * part].wait()
        copies[2 * part + 1].wait()
        for leaf in range(part * step, (part + 1) * step):
            exact.append(dot(basis[leaf], held[leaf]))
            leaf_out[leaf] = exact[leaf].astype(bf16)
    for tail in tails:
        tail.wait()
    for leaf, coefs in enumerate(exact):
        clusters[parent[leaf]] += dot_t(up_held[leaf], coefs, highest)
    total = dot_t(root_held[0], clusters[0], highest)
    for cluster in range(1, root_held.shape[0]):
        total = total + dot_t(root_held[cluster], clusters[cluster], highest)
    root_out[...] = total


def leaf_coefficients(local_parent, panels, bases, up_transfer, root_transfer):
    leaves, size, rhs = panels.shape
    rank = bases.shape[1]
    return pl.pallas_call(
        coefs_kernel,
        out_shape=(
            jax.ShapeDtypeStruct((leaves, rank, rhs), bf16),
            jax.ShapeDtypeStruct((rank, rhs), f32),
        ),
        in_specs=[scalars()] + [anywhere()] * 4,
        out_specs=(whole(), whole()),
        scratch_shapes=[
            pltpu.VMEM((leaves, size, rhs), bf16),
            pltpu.VMEM((leaves, rank, size), bf16),
            pltpu.VMEM(up_transfer.shape, f32),
            pltpu.VMEM(root_transfer.shape, f32),
            pltpu.VMEM((root_transfer.shape[0], rank, rhs), f32),
            pltpu.SemaphoreType.DMA((4, 2)),
            pltpu.SemaphoreType.DMA((2,)),
        ],
        compiler_params=params(12),
        cost_estimate=cost(1000, 1000),
        name="coefs",
    )(local_parent, *[in_hbm(array) for array in (panels, bases, up_transfer, root_transfer)])


def tables_kernel(nodes, transfer, coupling, transfer_out, coupling_out, held, sems):
    parts = sems.shape[1]
    step = held.shape[1] // parts
    rank, size = held.shape[2:]
    ids = lax.broadcasted_iota(jnp.int32, (nodes.shape[0], size), 1)
    chosen = (ids == nodes[...]).astype(bf16)
    copies = []
    for kind, table in enumerate((transfer, coupling)):
        for part in range(parts):
            rows = pl.ds(part * step, step)
            copies.append(pltpu.make_async_copy(table.at[rows], held.at[kind, rows], sems.at[kind, part]))
    for copy in copies:
        copy.start()
    for kind, out in enumerate((transfer_out, coupling_out)):
        for part in range(parts):
            copies[kind * parts + part].wait()
            first = part * step
            values = held[kind, first : first + step].reshape(-1, size)
            high = values.astype(bf16)
            low = (values - high.astype(f32)).astype(bf16)
            rows = dot_r(chosen, high) + dot_r(chosen, low)
            for row in range(step):
                out[:, first + row, :] = rows[:, row * rank : (row + 1) * rank]


def tables(nodes, transfer, coupling):
    count = nodes.shape[0]
    size, rank, _ = transfer.shape
    return pl.pallas_call(
        tables_kernel,
        out_shape=(jax.ShapeDtypeStruct((count, rank, rank), f32),) * 2,
        in_specs=[whole(), anywhere(), anywhere()],
        out_specs=(whole(),) * 2,
        scratch_shapes=[pltpu.VMEM((2, rank, rank, size), f32), pltpu.SemaphoreType.DMA((2, 8))],
        compiler_params=params(20),
        cost_estimate=cost(1000, 1000),
        name="tables",
    )(nodes, in_hbm(transfer.transpose(1, 2, 0)), in_hbm(coupling.transpose(1, 2, 0)))


def combine_kernel(own, other, current, sibling, mats, out):
    total = dot_t(mats[own], current[...], highest)
    out[...] = total + dot_t(mats[other], sibling[...], highest)


def combine(own, other, current, sibling, mats):
    return pl.pallas_call(
        lambda *refs: combine_kernel(own, other, *refs),
        out_shape=jax.ShapeDtypeStruct(current.shape, f32),
        in_specs=[whole(), whole(), whole()],
        out_specs=whole(),
        compiler_params=params(4),
        cost_estimate=cost(1000, 1000),
        name="combine",
    )(current, sibling, mats)


def combine_four_kernel(picks, root, one, two, three, mats, sibling_out, out):
    own, other, second, third, own_up, other_up = picks
    sibling = dot_t(mats[second], two[...], highest) + dot_t(mats[third], three[...], highest)
    sibling_out[...] = sibling
    lower = dot_t(mats[own], root[...], highest) + dot_t(mats[other], one[...], highest)
    out[...] = dot_t(mats[own_up], lower, highest) + dot_t(mats[other_up], sibling, highest)


def combine_four(picks, roots, mats):
    return pl.pallas_call(
        lambda *refs: combine_four_kernel(picks, *refs),
        out_shape=(jax.ShapeDtypeStruct(roots[0].shape, f32),) * 2,
        in_specs=[whole()] * 5,
        out_specs=(whole(),) * 2,
        compiler_params=params(2),
        cost_estimate=cost(1000, 1000),
        name="combine_four",
    )(*roots, mats)


def downward_kernel(depth, parent, *refs):
    siblings = refs[:depth]
    transfer, coupling, root, up, out, clusters = refs[depth:]
    down = dot(coupling[depth - 1], siblings[depth - 1][...], highest)
    for level in reversed(range(depth - 1)):
        across = dot(coupling[level], siblings[level][...], highest)
        down = across + dot(transfer[level], down, highest)
    for cluster in range(root.shape[0]):
        clusters[cluster] = dot(root[cluster], down, highest)
    for leaf in range(up.shape[0]):
        out[leaf] = dot(up[leaf], clusters[parent[leaf]], highest)


def downward(local_parent, siblings, transfer, coupling, root_transfer, up_transfer):
    depth = len(siblings)
    rank, rhs = siblings[0].shape
    return pl.pallas_call(
        lambda *refs: downward_kernel(depth, *refs),
        out_shape=jax.ShapeDtypeStruct((up_transfer.shape[0], rank, rhs), f32),
        in_specs=[scalars()] + [whole()] * (depth + 4),
        out_specs=whole(),
        scratch_shapes=[pltpu.VMEM((root_transfer.shape[0], rank, rhs), f32)],
        compiler_params=params(16),
        cost_estimate=cost(1000, 1000),
        name="downward",
    )(local_parent, *siblings, transfer, coupling, root_transfer, up_transfer)


def weights_kernel(count, coupling, out, held, sems):
    leaves, slots, _, rank = coupling.shape
    copies = [pltpu.make_async_copy(coupling.at[leaf], held.at[leaf], sems.at[leaf]) for leaf in range(leaves)]
    for copy in copies:
        copy.start()
    for leaf in range(leaves):
        used = count[leaf]
        copies[leaf].wait()
        for pair in range(slots // 2):
            left = jnp.where(2 * pair < used, held[leaf, 2 * pair], 0.0)
            right = jnp.where(2 * pair + 1 < used, held[leaf, 2 * pair + 1], 0.0)
            joined = jnp.concatenate([left, right], axis=1).astype(bf16)
            out[leaf, :, 2 * pair * rank : 2 * (pair + 1) * rank] = joined


def weights(far_count, far_coupling):
    leaves, slots, rank, _ = far_coupling.shape
    return pl.pallas_call(
        weights_kernel,
        out_shape=jax.ShapeDtypeStruct((leaves, rank, slots * rank), bf16),
        in_specs=[scalars(), anywhere()],
        out_specs=whole(),
        scratch_shapes=[pltpu.VMEM(far_coupling.shape, f32), pltpu.SemaphoreType.DMA((leaves,))],
        compiler_params=params(20),
        cost_estimate=cost(1000, 1000),
        name="weights",
    )(far_count, in_hbm(far_coupling))


def near_kernel(position, blocks, *refs):
    pieces = refs[:-7]
    out, held, matrices, piece_sems, block_sems, sums, out_sems = refs[-7:]
    leaves, slots = blocks.shape[:2]
    copies = []
    first = 0
    for index, piece in enumerate(pieces):
        rows = pl.ds(first, piece.shape[0])
        copies.append(pltpu.make_async_copy(piece, held.at[rows], piece_sems.at[index]))
        first += piece.shape[0]
    fetches = [
        pltpu.make_async_copy(blocks.at[leaf], matrices.at[leaf], block_sems.at[leaf]) for leaf in range(leaves)
    ]
    for copy in copies + fetches[:1]:
        copy.start()
    for copy in copies:
        copy.wait()
    for fetch in fetches[1:]:
        fetch.start()
    stores = []
    for leaf in range(leaves):
        fetches[leaf].wait()
        wide = jnp.concatenate([matrices[leaf, slot] for slot in range(slots)], axis=1)
        tall = jnp.concatenate([held[position[leaf * slots + slot]] for slot in range(slots)], axis=0)
        sums[leaf] = dot(wide, tall)
        stores.append(pltpu.make_async_copy(sums.at[leaf], out.at[leaf], out_sems.at[leaf]))
        stores[leaf].start()
    for store in stores:
        store.wait()


def near(position, near_blocks, pieces):
    leaves, slots, size, _ = near_blocks.shape
    rhs = pieces[0].shape[2]
    return pl.pallas_call(
        near_kernel,
        out_shape=pltpu.HBM((leaves, size, rhs), f32),
        in_specs=[scalars()] + [anywhere()] * (1 + len(pieces)),
        out_specs=pl.BlockSpec(memory_space=pltpu.HBM),
        scratch_shapes=[
            pltpu.VMEM((sum(piece.shape[0] for piece in pieces), size, rhs), bf16),
            pltpu.VMEM(near_blocks.shape, bf16),
            pltpu.SemaphoreType.DMA((len(pieces),)),
            pltpu.SemaphoreType.DMA((leaves,)),
            pltpu.VMEM((leaves, size, rhs), f32),
            pltpu.SemaphoreType.DMA((leaves,)),
        ],
        compiler_params=params(36),
        cost_estimate=cost(1000, 1000),
        name="near",
    )(position, in_hbm(near_blocks), *pieces)


def final_kernel(rows, packed, coefs, on_leaf, bases, near_part, out, *scratch):
    held, picked, results, term, basis, close, load_sems, near_sems, out_sems = scratch
    leaves, rank, wide = packed.shape
    slots = wide // rank
    loads = [
        pltpu.make_async_copy(source, target, load_sems.at[index])
        for index, (source, target) in enumerate(((coefs, held), (on_leaf, term), (bases, basis)))
    ]
    nears = [pltpu.make_async_copy(near_part.at[leaf], close.at[leaf], near_sems.at[leaf]) for leaf in range(leaves)]
    for load in loads:
        load.start()
    for load in loads:
        load.wait()
    for load in nears:
        load.start()
    stores = []
    for leaf in range(leaves):
        for slot in range(slots):
            picked[leaf, slot * rank : (slot + 1) * rank] = held[rows[leaf * slots + slot]]
        expansion = (term[leaf] + dot(packed[leaf], picked[leaf])).astype(bf16)
        nears[leaf].wait()
        results[leaf] = (dot_t(basis[leaf], expansion) + close[leaf]).astype(bf16)
        stores.append(pltpu.make_async_copy(results.at[leaf], out.at[leaf], out_sems.at[leaf]))
        stores[leaf].start()
    for store in stores:
        store.wait()


def final(far_rows, packed, slab_coefs, on_leaf, bases, near_part):
    leaves, rank, size = bases.shape
    rhs = near_part.shape[2]
    wide = packed.shape[2]
    return pl.pallas_call(
        final_kernel,
        out_shape=jax.ShapeDtypeStruct((leaves, size, rhs), bf16),
        in_specs=[scalars(), whole()] + [anywhere()] * 4,
        out_specs=anywhere(),
        scratch_shapes=[
            pltpu.VMEM(slab_coefs.shape, bf16),
            pltpu.VMEM((leaves, wide, rhs), bf16),
            pltpu.VMEM((leaves, size, rhs), bf16),
            pltpu.VMEM(on_leaf.shape, f32),
            pltpu.VMEM(bases.shape, bf16),
            pltpu.VMEM(near_part.shape, f32),
            pltpu.SemaphoreType.DMA((3,)),
            pltpu.SemaphoreType.DMA((leaves,)),
            pltpu.SemaphoreType.DMA((leaves,)),
        ],
        compiler_params=params(24),
        cost_estimate=cost(1000, 1000),
        name="final",
    )(far_rows, packed, in_hbm(slab_coefs), on_leaf, in_hbm(bases), in_hbm(near_part))


def shifted(array, axis, step, closed):
    count = lax.axis_size(axis)
    pairs = [(i, (i + step) % count) for i in range(count) if closed or 0 <= i + step < count]
    return lax.ppermute(array, axis, pairs)


def both(array, axis, closed):
    return shifted(array, axis, 1, closed), shifted(array, axis, -1, closed)


def after(*arrays):
    return lax.optimization_barrier(arrays)


def partner(array, axis, flip):
    return lax.ppermute(array, axis, [(i, i ^ flip) for i in range(lax.axis_size(axis))])


def local(
    sources,
    bases,
    leaf_parent,
    up_transfer,
    root_transfer,
    top_transfer,
    top_coupling,
    near_list,
    near_blocks,
    far_list,
    far_count,
    far_coupling,
):
    leaf_total, leaf_size, _ = bases.shape
    bases = bases.transpose(0, 2, 1)
    rhs_count = sources.shape[1]
    cluster_total = leaf_total // 2
    slab_count = lax.axis_size("slab")
    sector_count = lax.axis_size("sector")
    devices = slab_count * sector_count
    depth = devices.bit_length() - 1
    slab_pos = lax.axis_index("slab")
    sector_pos = lax.axis_index("sector")
    device = slab_pos * sector_count + sector_pos
    panels = sources.reshape(leaf_total, leaf_size, rhs_count)

    local_parent = leaf_parent - device * cluster_total
    leaf_coefs, root = leaf_coefficients(local_parent, panels, bases, up_transfer, root_transfer)
    slab_coefs = lax.all_gather(leaf_coefs, "sector", axis=0, tiled=True)

    owner_device = near_list // leaf_total
    slab_offset = (owner_device // sector_count - slab_pos) % 3
    sector_offset = (owner_device % sector_count - sector_pos) % sector_count
    row = jnp.where(sector_offset == 0, 0, jnp.where(sector_offset == 1, 6, 3)) + slab_offset
    position = (row * leaf_total + near_list % leaf_total).reshape(-1)
    far_rows = (far_list - slab_pos * (sector_count * leaf_total)).reshape(-1)

    both_axes = ("slab", "sector")
    quad = [root] + [partner(root, both_axes, flip) for flip in (1, 2, 3)]
    shared, *quad = after(panels, *quad)
    sides = both(shared, "sector", True)
    later, position, far_rows = after(panels, position, far_rows)
    below, above = both(later, "slab", False)
    slots = jnp.arange(2 * depth + 2, dtype=jnp.int32)
    level_of = jnp.where(slots < 2 * depth, slots % depth, 0)
    flips = jnp.where(slots < 2 * depth, slots // depth, 2 + slots % 2)
    nodes = ((devices + device) >> level_of) ^ flips
    nodes, position, far_rows, *quad = after(nodes, position, far_rows, *quad)
    transfer, coupling = tables(nodes[:, None], top_transfer, top_coupling)

    picks = (0, depth, 2 * depth, 2 * depth + 1, 1, depth + 1)
    across, current = combine_four(picks, quad, transfer)
    siblings = [quad[1], across]
    packed = weights(far_count, far_coupling)
    for level in range(2, depth):
        sibling = partner(current, both_axes, 1 << level)
        if level == 2:
            current, sibling, packed, below, above, *sides = after(current, sibling, packed, below, above, *sides)
            corners = [both(side, "slab", False) for side in sides]
            pieces = [panels, above, below]
            for side, corner in zip(sides, corners):
                pieces += [side, corner[1], corner[0]]
        if level == depth - 2:
            near_part = near(position, near_blocks, pieces)
            current, sibling, near_part = after(current, sibling, near_part)
        siblings.append(sibling)
        if level < depth - 1:
            current = combine(level, depth + level, current, sibling, transfer)
    on_leaf = downward(local_parent, siblings, transfer, coupling, root_transfer, up_transfer)
    field = final(far_rows, packed, slab_coefs, on_leaf, bases, near_part)
    return field.reshape(leaf_total * leaf_size, rhs_count)


def solution(mesh):
    placed = (
        P(("slab", "sector"), None),
        P(("slab", "sector"), None, None),
        P(("slab", "sector")),
        P(("slab", "sector"), None, None),
        P(("slab", "sector"), None, None),
        P(),
        P(),
        P(("slab", "sector"), None),
        P(("slab", "sector"), None, None, None),
        P(("slab", "sector"), None),
        P(("slab", "sector")),
        P(("slab", "sector"), None, None, None),
    )
    return jax.shard_map(
        local, mesh=mesh, in_specs=placed, out_specs=P(("slab", "sector"), None), check_vma=False
    )
```

```python
import jax
import jax.numpy as jnp
from jax import lax
from jax.experimental import pallas as pl
from jax.experimental.pallas import tpu as pltpu
from jax.sharding import PartitionSpec as P

highest = lax.Precision.HIGHEST
f32 = jnp.float32
bf16 = jnp.bfloat16


def dot_t(a, b, precision=None):
    return lax.dot_general(a, b, (((0,), (0,)), ((), ())), precision=precision, preferred_element_type=f32)


def dot(a, b, precision=None):
    return lax.dot_general(a, b, (((1,), (0,)), ((), ())), precision=precision, preferred_element_type=f32)


def dot_r(a, b):
    return lax.dot_general(a, b, (((1,), (1,)), ((), ())), preferred_element_type=f32)


def in_hbm(array):
    return pltpu.with_memory_space_constraint(array, pltpu.HBM)


def whole():
    return pl.BlockSpec(memory_space=pltpu.VMEM)


def anywhere():
    return pl.BlockSpec(memory_space=pl.ANY)


def scalars():
    return pl.BlockSpec(memory_space=pltpu.SMEM)


def params(mib, semantics=None):
    return pltpu.CompilerParams(vmem_limit_bytes=mib << 20, dimension_semantics=semantics)


def cost(flops, nbytes):
    return pl.CostEstimate(flops=flops, bytes_accessed=nbytes, transcendentals=0)


def coefs_kernel(parent, sources, bases, up, root, leaf_out, root_out, held, basis, up_held, root_held, clusters, sems, tail_sems):
    group = sems.shape[0]
    step = held.shape[0] // group
    copies = []
    for part in range(group):
        rows = pl.ds(part * step, step)
        copies.append(pltpu.make_async_copy(sources.at[rows], held.at[rows], sems.at[part, 0]))
        copies.append(pltpu.make_async_copy(bases.at[rows], basis.at[rows], sems.at[part, 1]))
    tails = [
        pltpu.make_async_copy(up, up_held, tail_sems.at[0]),
        pltpu.make_async_copy(root, root_held, tail_sems.at[1]),
    ]
    for copy in copies + tails:
        copy.start()
    clusters[...] = jnp.zeros_like(clusters)
    exact = []
    for part in range(group):
        copies[2 * part].wait()
        copies[2 * part + 1].wait()
        for leaf in range(part * step, (part + 1) * step):
            exact.append(dot(basis[leaf], held[leaf]))
            leaf_out[leaf] = exact[leaf].astype(bf16)
    for tail in tails:
        tail.wait()
    for leaf, coefs in enumerate(exact):
        clusters[parent[leaf]] += dot_t(up_held[leaf], coefs, highest)
    total = dot_t(root_held[0], clusters[0], highest)
    for cluster in range(1, root_held.shape[0]):
        total = total + dot_t(root_held[cluster], clusters[cluster], highest)
    root_out[...] = total


def leaf_coefficients(local_parent, panels, bases, up_transfer, root_transfer):
    leaves, size, rhs = panels.shape
    rank = bases.shape[1]
    return pl.pallas_call(
        coefs_kernel,
        out_shape=(
            jax.ShapeDtypeStruct((leaves, rank, rhs), bf16),
            jax.ShapeDtypeStruct((rank, rhs), f32),
        ),
        in_specs=[scalars()] + [anywhere()] * 4,
        out_specs=(whole(), whole()),
        scratch_shapes=[
            pltpu.VMEM((leaves, size, rhs), bf16),
            pltpu.VMEM((leaves, rank, size), bf16),
            pltpu.VMEM(up_transfer.shape, f32),
            pltpu.VMEM(root_transfer.shape, f32),
            pltpu.VMEM((root_transfer.shape[0], rank, rhs), f32),
            pltpu.SemaphoreType.DMA((4, 2)),
            pltpu.SemaphoreType.DMA((2,)),
        ],
        compiler_params=params(12),
        cost_estimate=cost(1000, 1000),
        name="coefs",
    )(local_parent, *[in_hbm(array) for array in (panels, bases, up_transfer, root_transfer)])


def tables_kernel(nodes, transfer, coupling, transfer_out, coupling_out, held, sems):
    parts = sems.shape[1]
    step = held.shape[1] // parts
    rank, size = held.shape[2:]
    ids = lax.broadcasted_iota(jnp.int32, (nodes.shape[0], size), 1)
    chosen = (ids == nodes[...]).astype(bf16)
    copies = []
    for kind, table in enumerate((transfer, coupling)):
        for part in range(parts):
            rows = pl.ds(part * step, step)
            copies.append(pltpu.make_async_copy(table.at[rows], held.at[kind, rows], sems.at[kind, part]))
    for copy in copies:
        copy.start()
    for kind, out in enumerate((transfer_out, coupling_out)):
        for part in range(parts):
            copies[kind * parts + part].wait()
            first = part * step
            values = held[kind, first : first + step].reshape(-1, size)
            high = values.astype(bf16)
            low = (values - high.astype(f32)).astype(bf16)
            rows = dot_r(chosen, high) + dot_r(chosen, low)
            for row in range(step):
                out[:, first + row, :] = rows[:, row * rank : (row + 1) * rank]


def tables(nodes, transfer, coupling):
    count = nodes.shape[0]
    size, rank, _ = transfer.shape
    return pl.pallas_call(
        tables_kernel,
        out_shape=(jax.ShapeDtypeStruct((count, rank, rank), f32),) * 2,
        in_specs=[whole(), anywhere(), anywhere()],
        out_specs=(whole(),) * 2,
        scratch_shapes=[pltpu.VMEM((2, rank, rank, size), f32), pltpu.SemaphoreType.DMA((2, 8))],
        compiler_params=params(20),
        cost_estimate=cost(1000, 1000),
        name="tables",
    )(nodes, in_hbm(transfer.transpose(1, 2, 0)), in_hbm(coupling.transpose(1, 2, 0)))


def combine_kernel(own, other, current, sibling, mats, out):
    total = dot_t(mats[own], current[...], highest)
    out[...] = total + dot_t(mats[other], sibling[...], highest)


def combine(own, other, current, sibling, mats):
    return pl.pallas_call(
        lambda *refs: combine_kernel(own, other, *refs),
        out_shape=jax.ShapeDtypeStruct(current.shape, f32),
        in_specs=[whole(), whole(), whole()],
        out_specs=whole(),
        compiler_params=params(4),
        cost_estimate=cost(1000, 1000),
        name="combine",
    )(current, sibling, mats)


def combine_four_kernel(picks, root, one, two, three, mats, sibling_out, out):
    own, other, second, third, own_up, other_up = picks
    sibling = dot_t(mats[second], two[...], highest) + dot_t(mats[third], three[...], highest)
    sibling_out[...] = sibling
    lower = dot_t(mats[own], root[...], highest) + dot_t(mats[other], one[...], highest)
    out[...] = dot_t(mats[own_up], lower, highest) + dot_t(mats[other_up], sibling, highest)


def combine_four(picks, roots, mats):
    return pl.pallas_call(
        lambda *refs: combine_four_kernel(picks, *refs),
        out_shape=(jax.ShapeDtypeStruct(roots[0].shape, f32),) * 2,
        in_specs=[whole()] * 5,
        out_specs=(whole(),) * 2,
        compiler_params=params(2),
        cost_estimate=cost(1000, 1000),
        name="combine_four",
    )(*roots, mats)


def downward_kernel(depth, parent, *refs):
    siblings = refs[:depth]
    transfer, coupling, root, up, out, clusters = refs[depth:]
    down = dot(coupling[depth - 1], siblings[depth - 1][...], highest)
    for level in reversed(range(depth - 1)):
        across = dot(coupling[level], siblings[level][...], highest)
        down = across + dot(transfer[level], down, highest)
    for cluster in range(root.shape[0]):
        clusters[cluster] = dot(root[cluster], down, highest)
    for leaf in range(up.shape[0]):
        out[leaf] = dot(up[leaf], clusters[parent[leaf]], highest)


def downward(local_parent, siblings, transfer, coupling, root_transfer, up_transfer):
    depth = len(siblings)
    rank, rhs = siblings[0].shape
    return pl.pallas_call(
        lambda *refs: downward_kernel(depth, *refs),
        out_shape=jax.ShapeDtypeStruct((up_transfer.shape[0], rank, rhs), f32),
        in_specs=[scalars()] + [whole()] * (depth + 4),
        out_specs=whole(),
        scratch_shapes=[pltpu.VMEM((root_transfer.shape[0], rank, rhs), f32)],
        compiler_params=params(16),
        cost_estimate=cost(1000, 1000),
        name="downward",
    )(local_parent, *siblings, transfer, coupling, root_transfer, up_transfer)


def weights_kernel(count, coupling, out, held, sems):
    leaves, slots, _, rank = coupling.shape
    copies = [pltpu.make_async_copy(coupling.at[leaf], held.at[leaf], sems.at[leaf]) for leaf in range(leaves)]
    for copy in copies:
        copy.start()
    for leaf in range(leaves):
        used = count[leaf]
        copies[leaf].wait()
        for pair in range(slots // 2):
            left = jnp.where(2 * pair < used, held[leaf, 2 * pair], 0.0)
            right = jnp.where(2 * pair + 1 < used, held[leaf, 2 * pair + 1], 0.0)
            joined = jnp.concatenate([left, right], axis=1).astype(bf16)
            out[leaf, :, 2 * pair * rank : 2 * (pair + 1) * rank] = joined


def weights(far_count, far_coupling):
    leaves, slots, rank, _ = far_coupling.shape
    return pl.pallas_call(
        weights_kernel,
        out_shape=jax.ShapeDtypeStruct((leaves, rank, slots * rank), bf16),
        in_specs=[scalars(), anywhere()],
        out_specs=whole(),
        scratch_shapes=[pltpu.VMEM(far_coupling.shape, f32), pltpu.SemaphoreType.DMA((leaves,))],
        compiler_params=params(20),
        cost_estimate=cost(1000, 1000),
        name="weights",
    )(far_count, in_hbm(far_coupling))


def near_kernel(position, blocks, *refs):
    pieces = refs[:-7]
    out, held, matrices, piece_sems, block_sems, sums, out_sems = refs[-7:]
    leaves, slots = blocks.shape[:2]
    copies = []
    first = 0
    for index, piece in enumerate(pieces):
        rows = pl.ds(first, piece.shape[0])
        copies.append(pltpu.make_async_copy(piece, held.at[rows], piece_sems.at[index]))
        first += piece.shape[0]
    fetches = [
        pltpu.make_async_copy(blocks.at[leaf], matrices.at[leaf], block_sems.at[leaf]) for leaf in range(leaves)
    ]
    for copy in copies + fetches[:1]:
        copy.start()
    for copy in copies:
        copy.wait()
    for fetch in fetches[1:]:
        fetch.start()
    stores = []
    for leaf in range(leaves):
        fetches[leaf].wait()
        wide = jnp.concatenate([matrices[leaf, slot] for slot in range(slots)], axis=1)
        tall = jnp.concatenate([held[position[leaf * slots + slot]] for slot in range(slots)], axis=0)
        sums[leaf] = dot(wide, tall)
        stores.append(pltpu.make_async_copy(sums.at[leaf], out.at[leaf], out_sems.at[leaf]))
        stores[leaf].start()
    for store in stores:
        store.wait()


def near(position, near_blocks, pieces):
    leaves, slots, size, _ = near_blocks.shape
    rhs = pieces[0].shape[2]
    return pl.pallas_call(
        near_kernel,
        out_shape=pltpu.HBM((leaves, size, rhs), f32),
        in_specs=[scalars()] + [anywhere()] * (1 + len(pieces)),
        out_specs=pl.BlockSpec(memory_space=pltpu.HBM),
        scratch_shapes=[
            pltpu.VMEM((sum(piece.shape[0] for piece in pieces), size, rhs), bf16),
            pltpu.VMEM(near_blocks.shape, bf16),
            pltpu.SemaphoreType.DMA((len(pieces),)),
            pltpu.SemaphoreType.DMA((leaves,)),
            pltpu.VMEM((leaves, size, rhs), f32),
            pltpu.SemaphoreType.DMA((leaves,)),
        ],
        compiler_params=params(36),
        cost_estimate=cost(1000, 1000),
        name="near",
    )(position, in_hbm(near_blocks), *pieces)


def final_kernel(rows, packed, coefs, on_leaf, bases, near_part, out, *scratch):
    held, picked, results, term, basis, close, load_sems, near_sems, out_sems = scratch
    leaves, rank, wide = packed.shape
    slots = wide // rank
    loads = [
        pltpu.make_async_copy(source, target, load_sems.at[index])
        for index, (source, target) in enumerate(((coefs, held), (on_leaf, term), (bases, basis)))
    ]
    nears = [pltpu.make_async_copy(near_part.at[leaf], close.at[leaf], near_sems.at[leaf]) for leaf in range(leaves)]
    loads[0].start()
    loads[0].wait()
    for load in loads[1:] + nears:
        load.start()
    stores = []
    for leaf in range(leaves):
        for slot in range(slots):
            picked[leaf, slot * rank : (slot + 1) * rank] = held[rows[leaf * slots + slot]]
        if leaf == 0:
            loads[1].wait()
            loads[2].wait()
        expansion = (term[leaf] + dot(packed[leaf], picked[leaf])).astype(bf16)
        nears[leaf].wait()
        results[leaf] = (dot_t(basis[leaf], expansion) + close[leaf]).astype(bf16)
        stores.append(pltpu.make_async_copy(results.at[leaf], out.at[leaf], out_sems.at[leaf]))
        stores[leaf].start()
    for store in stores:
        store.wait()


def final(far_rows, packed, slab_coefs, on_leaf, bases, near_part):
    leaves, rank, size = bases.shape
    rhs = near_part.shape[2]
    wide = packed.shape[2]
    return pl.pallas_call(
        final_kernel,
        out_shape=jax.ShapeDtypeStruct((leaves, size, rhs), bf16),
        in_specs=[scalars(), whole()] + [anywhere()] * 4,
        out_specs=anywhere(),
        scratch_shapes=[
            pltpu.VMEM(slab_coefs.shape, bf16),
            pltpu.VMEM((leaves, wide, rhs), bf16),
            pltpu.VMEM((leaves, size, rhs), bf16),
            pltpu.VMEM(on_leaf.shape, f32),
            pltpu.VMEM(bases.shape, bf16),
            pltpu.VMEM(near_part.shape, f32),
            pltpu.SemaphoreType.DMA((3,)),
            pltpu.SemaphoreType.DMA((leaves,)),
            pltpu.SemaphoreType.DMA((leaves,)),
        ],
        compiler_params=params(24),
        cost_estimate=cost(1000, 1000),
        name="final",
    )(far_rows, packed, in_hbm(slab_coefs), on_leaf, in_hbm(bases), in_hbm(near_part))


def shifted(array, axis, step, closed):
    count = lax.axis_size(axis)
    pairs = [(i, (i + step) % count) for i in range(count) if closed or 0 <= i + step < count]
    return lax.ppermute(array, axis, pairs)


def both(array, axis, closed):
    return shifted(array, axis, 1, closed), shifted(array, axis, -1, closed)


def after(*arrays):
    return lax.optimization_barrier(arrays)


def partner(array, axis, flip):
    return lax.ppermute(array, axis, [(i, i ^ flip) for i in range(lax.axis_size(axis))])


def local(
    sources,
    bases,
    leaf_parent,
    up_transfer,
    root_transfer,
    top_transfer,
    top_coupling,
    near_list,
    near_blocks,
    far_list,
    far_count,
    far_coupling,
):
    leaf_total, leaf_size, _ = bases.shape
    bases = bases.transpose(0, 2, 1)
    rhs_count = sources.shape[1]
    cluster_total = leaf_total // 2
    slab_count = lax.axis_size("slab")
    sector_count = lax.axis_size("sector")
    devices = slab_count * sector_count
    depth = devices.bit_length() - 1
    slab_pos = lax.axis_index("slab")
    sector_pos = lax.axis_index("sector")
    device = slab_pos * sector_count + sector_pos
    panels = sources.reshape(leaf_total, leaf_size, rhs_count)

    local_parent = leaf_parent - device * cluster_total
    leaf_coefs, root = leaf_coefficients(local_parent, panels, bases, up_transfer, root_transfer)
    slab_coefs = lax.all_gather(leaf_coefs, "sector", axis=0, tiled=True)

    owner_device = near_list // leaf_total
    slab_offset = (owner_device // sector_count - slab_pos) % 3
    sector_offset = (owner_device % sector_count - sector_pos) % sector_count
    row = jnp.where(sector_offset == 0, 0, jnp.where(sector_offset == 1, 6, 3)) + slab_offset
    position = (row * leaf_total + near_list % leaf_total).reshape(-1)
    far_rows = (far_list - slab_pos * (sector_count * leaf_total)).reshape(-1)

    both_axes = ("slab", "sector")
    sides = both(panels, "sector", True)
    slots = jnp.arange(2 * depth + 2, dtype=jnp.int32)
    level_of = jnp.where(slots < 2 * depth, slots % depth, 0)
    flips = jnp.where(slots < 2 * depth, slots // depth, 2 + slots % 2)
    nodes = ((devices + device) >> level_of) ^ flips
    transfer, coupling = tables(nodes[:, None], top_transfer, top_coupling)
    below, above = both(panels, "slab", False)
    packed = weights(far_count, far_coupling)

    root, below, above, packed, transfer, position, far_rows = after(
        root, below, above, packed, transfer, position, far_rows
    )
    quad = [root] + [partner(root, both_axes, flip) for flip in (1, 2, 3)]
    flat = after(*quad, *sides)
    quad, sides = flat[:4], flat[4:]
    corners = [both(side, "slab", False) for side in sides]
    pieces = [panels, above, below]
    for side, corner in zip(sides, corners):
        pieces += [side, corner[1], corner[0]]
    picks = (0, depth, 2 * depth, 2 * depth + 1, 1, depth + 1)
    across, current = combine_four(picks, quad, transfer)
    siblings = [quad[1], across]
    for level in range(2, depth):
        sibling = partner(current, both_axes, 1 << level)
        if level == depth - 2:
            near_part = near(position, near_blocks, pieces)
            current, sibling, near_part = after(current, sibling, near_part)
        siblings.append(sibling)
        if level < depth - 1:
            current = combine(level, depth + level, current, sibling, transfer)
    on_leaf = downward(local_parent, siblings, transfer, coupling, root_transfer, up_transfer)
    field = final(far_rows, packed, slab_coefs, on_leaf, bases, near_part)
    return field.reshape(leaf_total * leaf_size, rhs_count)


def solution(mesh):
    placed = (
        P(("slab", "sector"), None),
        P(("slab", "sector"), None, None),
        P(("slab", "sector")),
        P(("slab", "sector"), None, None),
        P(("slab", "sector"), None, None),
        P(),
        P(),
        P(("slab", "sector"), None),
        P(("slab", "sector"), None, None, None),
        P(("slab", "sector"), None),
        P(("slab", "sector")),
        P(("slab", "sector"), None, None, None),
    )
    return jax.shard_map(
        local, mesh=mesh, in_specs=placed, out_specs=P(("slab", "sector"), None), check_vma=False
    )
```

```python
import jax
import jax.numpy as jnp
from jax import lax
from jax.experimental import pallas as pl
from jax.experimental.pallas import tpu as pltpu
from jax.sharding import PartitionSpec as P

f32 = jnp.float32
bf16 = jnp.bfloat16


def dot_t(a, b):
    return lax.dot_general(a, b, (((0,), (0,)), ((), ())), preferred_element_type=f32)


def dot(a, b):
    return lax.dot_general(a, b, (((1,), (0,)), ((), ())), preferred_element_type=f32)


def halves(a):
    high = a.astype(bf16)
    return high, (a - high.astype(f32)).astype(bf16)


def fine(product, a, b):
    (a_high, a_low), (b_high, b_low) = halves(a), halves(b)
    return product(a_high, b_high) + (product(a_high, b_low) + product(a_low, b_high))


def fine_t(a, b):
    return fine(dot_t, a, b)


def fine_dot(a, b):
    return fine(dot, a, b)


def dot_r(a, b):
    return lax.dot_general(a, b, (((1,), (1,)), ((), ())), preferred_element_type=f32)


def in_hbm(array):
    return pltpu.with_memory_space_constraint(array, pltpu.HBM)


def whole():
    return pl.BlockSpec(memory_space=pltpu.VMEM)


def anywhere():
    return pl.BlockSpec(memory_space=pl.ANY)


def scalars():
    return pl.BlockSpec(memory_space=pltpu.SMEM)


def params(mib, semantics=None):
    return pltpu.CompilerParams(vmem_limit_bytes=mib << 20, dimension_semantics=semantics)


def cost(flops, nbytes):
    return pl.CostEstimate(flops=flops, bytes_accessed=nbytes, transcendentals=0)


def coefs_kernel(parent, sources, bases, up, root, leaf_out, root_out, held, basis, up_held, root_held, clusters, sems, tail_sems):
    group = sems.shape[0]
    step = held.shape[0] // group
    copies = []
    for part in range(group):
        rows = pl.ds(part * step, step)
        copies.append(pltpu.make_async_copy(sources.at[rows], held.at[rows], sems.at[part, 0]))
        copies.append(pltpu.make_async_copy(bases.at[rows], basis.at[rows], sems.at[part, 1]))
    tails = [
        pltpu.make_async_copy(up, up_held, tail_sems.at[0]),
        pltpu.make_async_copy(root, root_held, tail_sems.at[1]),
    ]
    for copy in copies + tails:
        copy.start()
    clusters[...] = jnp.zeros_like(clusters)
    exact = []
    for part in range(group):
        copies[2 * part].wait()
        copies[2 * part + 1].wait()
        for leaf in range(part * step, (part + 1) * step):
            exact.append(dot(basis[leaf], held[leaf]))
            leaf_out[leaf] = exact[leaf].astype(bf16)
    for tail in tails:
        tail.wait()
    for leaf, coefs in enumerate(exact):
        clusters[parent[leaf]] += fine_t(up_held[leaf], coefs)
    total = fine_t(root_held[0], clusters[0])
    for cluster in range(1, root_held.shape[0]):
        total = total + fine_t(root_held[cluster], clusters[cluster])
    root_out[...] = total


def leaf_coefficients(local_parent, panels, bases, up_transfer, root_transfer):
    leaves, size, rhs = panels.shape
    rank = bases.shape[1]
    return pl.pallas_call(
        coefs_kernel,
        out_shape=(
            jax.ShapeDtypeStruct((leaves, rank, rhs), bf16),
            jax.ShapeDtypeStruct((rank, rhs), f32),
        ),
        in_specs=[scalars()] + [anywhere()] * 4,
        out_specs=(whole(), whole()),
        scratch_shapes=[
            pltpu.VMEM((leaves, size, rhs), bf16),
            pltpu.VMEM((leaves, rank, size), bf16),
            pltpu.VMEM(up_transfer.shape, f32),
            pltpu.VMEM(root_transfer.shape, f32),
            pltpu.VMEM((root_transfer.shape[0], rank, rhs), f32),
            pltpu.SemaphoreType.DMA((4, 2)),
            pltpu.SemaphoreType.DMA((2,)),
        ],
        compiler_params=params(12),
        cost_estimate=cost(1000, 1000),
        name="coefs",
    )(local_parent, *[in_hbm(array) for array in (panels, bases, up_transfer, root_transfer)])


def tables_kernel(nodes, transfer, coupling, transfer_out, coupling_out, held, sems):
    parts = sems.shape[1]
    step = held.shape[1] // parts
    rank, size = held.shape[2:]
    ids = lax.broadcasted_iota(jnp.int32, (nodes.shape[0], size), 1)
    chosen = (ids == nodes[...]).astype(bf16)
    copies = []
    for kind, table in enumerate((transfer, coupling)):
        for part in range(parts):
            rows = pl.ds(part * step, step)
            copies.append(pltpu.make_async_copy(table.at[rows], held.at[kind, rows], sems.at[kind, part]))
    for copy in copies:
        copy.start()
    for kind, out in enumerate((transfer_out, coupling_out)):
        for part in range(parts):
            copies[kind * parts + part].wait()
            first = part * step
            values = held[kind, first : first + step].reshape(-1, size)
            high = values.astype(bf16)
            low = (values - high.astype(f32)).astype(bf16)
            rows = dot_r(chosen, high) + dot_r(chosen, low)
            for row in range(step):
                out[:, first + row, :] = rows[:, row * rank : (row + 1) * rank]


def tables(nodes, transfer, coupling):
    count = nodes.shape[0]
    size, rank, _ = transfer.shape
    return pl.pallas_call(
        tables_kernel,
        out_shape=(jax.ShapeDtypeStruct((count, rank, rank), f32),) * 2,
        in_specs=[whole(), anywhere(), anywhere()],
        out_specs=(whole(),) * 2,
        scratch_shapes=[pltpu.VMEM((2, rank, rank, size), f32), pltpu.SemaphoreType.DMA((2, 8))],
        compiler_params=params(20),
        cost_estimate=cost(1000, 1000),
        name="tables",
    )(nodes, in_hbm(transfer.transpose(1, 2, 0)), in_hbm(coupling.transpose(1, 2, 0)))


def combine_kernel(own, other, current, sibling, mats, out):
    total = fine_t(mats[own], current[...])
    out[...] = total + fine_t(mats[other], sibling[...])


def combine(own, other, current, sibling, mats):
    return pl.pallas_call(
        lambda *refs: combine_kernel(own, other, *refs),
        out_shape=jax.ShapeDtypeStruct(current.shape, f32),
        in_specs=[whole(), whole(), whole()],
        out_specs=whole(),
        compiler_params=params(4),
        cost_estimate=cost(1000, 1000),
        name="combine",
    )(current, sibling, mats)


def combine_four_kernel(picks, root, one, two, three, mats, sibling_out, out):
    own, other, second, third, own_up, other_up = picks
    sibling = fine_t(mats[second], two[...]) + fine_t(mats[third], three[...])
    sibling_out[...] = sibling
    lower = fine_t(mats[own], root[...]) + fine_t(mats[other], one[...])
    out[...] = fine_t(mats[own_up], lower) + fine_t(mats[other_up], sibling)


def combine_four(picks, roots, mats):
    return pl.pallas_call(
        lambda *refs: combine_four_kernel(picks, *refs),
        out_shape=(jax.ShapeDtypeStruct(roots[0].shape, f32),) * 2,
        in_specs=[whole()] * 5,
        out_specs=(whole(),) * 2,
        compiler_params=params(2),
        cost_estimate=cost(1000, 1000),
        name="combine_four",
    )(*roots, mats)


def downward_kernel(depth, parent, *refs):
    siblings = refs[:depth]
    transfer, coupling, root, up, out, clusters = refs[depth:]
    down = fine_dot(coupling[depth - 1], siblings[depth - 1][...])
    for level in reversed(range(depth - 1)):
        across = fine_dot(coupling[level], siblings[level][...])
        down = across + fine_dot(transfer[level], down)
    for cluster in range(root.shape[0]):
        clusters[cluster] = fine_dot(root[cluster], down)
    for leaf in range(up.shape[0]):
        out[leaf] = fine_dot(up[leaf], clusters[parent[leaf]])


def downward(local_parent, siblings, transfer, coupling, root_transfer, up_transfer):
    depth = len(siblings)
    rank, rhs = siblings[0].shape
    return pl.pallas_call(
        lambda *refs: downward_kernel(depth, *refs),
        out_shape=jax.ShapeDtypeStruct((up_transfer.shape[0], rank, rhs), f32),
        in_specs=[scalars()] + [whole()] * (depth + 4),
        out_specs=whole(),
        scratch_shapes=[pltpu.VMEM((root_transfer.shape[0], rank, rhs), f32)],
        compiler_params=params(16),
        cost_estimate=cost(1000, 1000),
        name="downward",
    )(local_parent, *siblings, transfer, coupling, root_transfer, up_transfer)


def weights_kernel(count, coupling, out, held, sems):
    leaves, slots, _, rank = coupling.shape
    copies = [pltpu.make_async_copy(coupling.at[leaf], held.at[leaf], sems.at[leaf]) for leaf in range(leaves)]
    for copy in copies:
        copy.start()
    for leaf in range(leaves):
        used = count[leaf]
        copies[leaf].wait()
        for pair in range(slots // 2):
            left = jnp.where(2 * pair < used, held[leaf, 2 * pair], 0.0)
            right = jnp.where(2 * pair + 1 < used, held[leaf, 2 * pair + 1], 0.0)
            joined = jnp.concatenate([left, right], axis=1).astype(bf16)
            out[leaf, :, 2 * pair * rank : 2 * (pair + 1) * rank] = joined


def weights(far_count, far_coupling):
    leaves, slots, rank, _ = far_coupling.shape
    return pl.pallas_call(
        weights_kernel,
        out_shape=jax.ShapeDtypeStruct((leaves, rank, slots * rank), bf16),
        in_specs=[scalars(), anywhere()],
        out_specs=whole(),
        scratch_shapes=[pltpu.VMEM(far_coupling.shape, f32), pltpu.SemaphoreType.DMA((leaves,))],
        compiler_params=params(20),
        cost_estimate=cost(1000, 1000),
        name="weights",
    )(far_count, in_hbm(far_coupling))


def near_kernel(position, blocks, *refs):
    pieces = refs[:-7]
    out, held, matrices, piece_sems, block_sems, sums, out_sems = refs[-7:]
    leaves, slots = blocks.shape[:2]
    copies = []
    first = 0
    for index, piece in enumerate(pieces):
        rows = pl.ds(first, piece.shape[0])
        copies.append(pltpu.make_async_copy(piece, held.at[rows], piece_sems.at[index]))
        first += piece.shape[0]
    fetches = [
        pltpu.make_async_copy(blocks.at[leaf], matrices.at[leaf], block_sems.at[leaf]) for leaf in range(leaves)
    ]
    for copy in copies + fetches[:1]:
        copy.start()
    for copy in copies:
        copy.wait()
    for fetch in fetches[1:]:
        fetch.start()
    stores = []
    for leaf in range(leaves):
        fetches[leaf].wait()
        wide = jnp.concatenate([matrices[leaf, slot] for slot in range(slots)], axis=1)
        tall = jnp.concatenate([held[position[leaf * slots + slot]] for slot in range(slots)], axis=0)
        sums[leaf] = dot(wide, tall)
        stores.append(pltpu.make_async_copy(sums.at[leaf], out.at[leaf], out_sems.at[leaf]))
        stores[leaf].start()
    for store in stores:
        store.wait()


def near(position, near_blocks, pieces):
    leaves, slots, size, _ = near_blocks.shape
    rhs = pieces[0].shape[2]
    return pl.pallas_call(
        near_kernel,
        out_shape=pltpu.HBM((leaves, size, rhs), f32),
        in_specs=[scalars()] + [anywhere()] * (1 + len(pieces)),
        out_specs=pl.BlockSpec(memory_space=pltpu.HBM),
        scratch_shapes=[
            pltpu.VMEM((sum(piece.shape[0] for piece in pieces), size, rhs), bf16),
            pltpu.VMEM(near_blocks.shape, bf16),
            pltpu.SemaphoreType.DMA((len(pieces),)),
            pltpu.SemaphoreType.DMA((leaves,)),
            pltpu.VMEM((leaves, size, rhs), f32),
            pltpu.SemaphoreType.DMA((leaves,)),
        ],
        compiler_params=params(36),
        cost_estimate=cost(1000, 1000),
        name="near",
    )(position, in_hbm(near_blocks), *pieces)


def final_kernel(rows, packed, coefs, on_leaf, bases, near_part, out, *scratch):
    held, picked, results, term, basis, close, load_sems, near_sems, out_sems = scratch
    leaves, rank, wide = packed.shape
    slots = wide // rank
    loads = [
        pltpu.make_async_copy(source, target, load_sems.at[index])
        for index, (source, target) in enumerate(((coefs, held), (on_leaf, term), (bases, basis)))
    ]
    nears = [pltpu.make_async_copy(near_part.at[leaf], close.at[leaf], near_sems.at[leaf]) for leaf in range(leaves)]
    for load in loads:
        load.start()
    for load in loads:
        load.wait()
    for load in nears:
        load.start()
    stores = []
    for leaf in range(leaves):
        for slot in range(slots):
            picked[leaf, slot * rank : (slot + 1) * rank] = held[rows[leaf * slots + slot]]
        expansion = (term[leaf] + dot(packed[leaf], picked[leaf])).astype(bf16)
        nears[leaf].wait()
        results[leaf] = (dot_t(basis[leaf], expansion) + close[leaf]).astype(bf16)
        stores.append(pltpu.make_async_copy(results.at[leaf], out.at[leaf], out_sems.at[leaf]))
        stores[leaf].start()
    for store in stores:
        store.wait()


def final(far_rows, packed, slab_coefs, on_leaf, bases, near_part):
    leaves, rank, size = bases.shape
    rhs = near_part.shape[2]
    wide = packed.shape[2]
    return pl.pallas_call(
        final_kernel,
        out_shape=jax.ShapeDtypeStruct((leaves, size, rhs), bf16),
        in_specs=[scalars(), whole()] + [anywhere()] * 4,
        out_specs=anywhere(),
        scratch_shapes=[
            pltpu.VMEM(slab_coefs.shape, bf16),
            pltpu.VMEM((leaves, wide, rhs), bf16),
            pltpu.VMEM((leaves, size, rhs), bf16),
            pltpu.VMEM(on_leaf.shape, f32),
            pltpu.VMEM(bases.shape, bf16),
            pltpu.VMEM(near_part.shape, f32),
            pltpu.SemaphoreType.DMA((3,)),
            pltpu.SemaphoreType.DMA((leaves,)),
            pltpu.SemaphoreType.DMA((leaves,)),
        ],
        compiler_params=params(24),
        cost_estimate=cost(1000, 1000),
        name="final",
    )(far_rows, packed, in_hbm(slab_coefs), on_leaf, in_hbm(bases), in_hbm(near_part))


def shifted(array, axis, step, closed):
    count = lax.axis_size(axis)
    pairs = [(i, (i + step) % count) for i in range(count) if closed or 0 <= i + step < count]
    return lax.ppermute(array, axis, pairs)


def both(array, axis, closed):
    return shifted(array, axis, 1, closed), shifted(array, axis, -1, closed)


def after(*arrays):
    return lax.optimization_barrier(arrays)


def partner(array, axis, flip):
    return lax.ppermute(array, axis, [(i, i ^ flip) for i in range(lax.axis_size(axis))])


def local(
    sources,
    bases,
    leaf_parent,
    up_transfer,
    root_transfer,
    top_transfer,
    top_coupling,
    near_list,
    near_blocks,
    far_list,
    far_count,
    far_coupling,
):
    leaf_total, leaf_size, _ = bases.shape
    bases = bases.transpose(0, 2, 1)
    rhs_count = sources.shape[1]
    cluster_total = leaf_total // 2
    slab_count = lax.axis_size("slab")
    sector_count = lax.axis_size("sector")
    devices = slab_count * sector_count
    depth = devices.bit_length() - 1
    slab_pos = lax.axis_index("slab")
    sector_pos = lax.axis_index("sector")
    device = slab_pos * sector_count + sector_pos
    panels = sources.reshape(leaf_total, leaf_size, rhs_count)

    local_parent = leaf_parent - device * cluster_total
    leaf_coefs, root = leaf_coefficients(local_parent, panels, bases, up_transfer, root_transfer)
    slab_coefs = lax.all_gather(leaf_coefs, "sector", axis=0, tiled=True)

    owner_device = near_list // leaf_total
    slab_offset = (owner_device // sector_count - slab_pos) % 3
    sector_offset = (owner_device % sector_count - sector_pos) % sector_count
    row = jnp.where(sector_offset == 0, 0, jnp.where(sector_offset == 1, 6, 3)) + slab_offset
    position = (row * leaf_total + near_list % leaf_total).reshape(-1)
    far_rows = (far_list - slab_pos * (sector_count * leaf_total)).reshape(-1)

    both_axes = ("slab", "sector")
    sides = both(panels, "sector", True)
    slots = jnp.arange(2 * depth + 2, dtype=jnp.int32)
    level_of = jnp.where(slots < 2 * depth, slots % depth, 0)
    flips = jnp.where(slots < 2 * depth, slots // depth, 2 + slots % 2)
    nodes = ((devices + device) >> level_of) ^ flips
    transfer, coupling = tables(nodes[:, None], top_transfer, top_coupling)
    below, above = both(panels, "slab", False)
    packed = weights(far_count, far_coupling)

    root, below, above, packed, transfer, position, far_rows = after(
        root, below, above, packed, transfer, position, far_rows
    )
    quad = [root] + [partner(root, both_axes, flip) for flip in (1, 2, 3)]
    flat = after(*quad, *sides)
    quad, sides = flat[:4], flat[4:]
    corners = [both(side, "slab", False) for side in sides]
    pieces = [in_hbm(panels), above, below]
    for side, corner in zip(sides, corners):
        pieces += [side, corner[1], corner[0]]
    picks = (0, depth, 2 * depth, 2 * depth + 1, 1, depth + 1)
    across, current = combine_four(picks, quad, transfer)
    siblings = [quad[1], across]
    for level in range(2, depth):
        sibling = partner(current, both_axes, 1 << level)
        if level == depth - 1:
            near_part = near(position, near_blocks, pieces)
            current, sibling, near_part = after(current, sibling, near_part)
        siblings.append(sibling)
        if level < depth - 1:
            current = combine(level, depth + level, current, sibling, transfer)
    on_leaf = downward(local_parent, siblings, transfer, coupling, root_transfer, up_transfer)
    field = final(far_rows, packed, slab_coefs, on_leaf, bases, near_part)
    return field.reshape(leaf_total * leaf_size, rhs_count)


def solution(mesh):
    placed = (
        P(("slab", "sector"), None),
        P(("slab", "sector"), None, None),
        P(("slab", "sector")),
        P(("slab", "sector"), None, None),
        P(("slab", "sector"), None, None),
        P(),
        P(),
        P(("slab", "sector"), None),
        P(("slab", "sector"), None, None, None),
        P(("slab", "sector"), None),
        P(("slab", "sector")),
        P(("slab", "sector"), None, None, None),
    )
    return jax.shard_map(
        local, mesh=mesh, in_specs=placed, out_specs=P(("slab", "sector"), None), check_vma=False
    )
```

```python
import jax
import jax.numpy as jnp
from jax import lax
from jax.experimental import pallas as pl
from jax.experimental.pallas import tpu as pltpu
from jax.sharding import PartitionSpec as P

f32 = jnp.float32
bf16 = jnp.bfloat16


def dot_t(a, b):
    return lax.dot_general(a, b, (((0,), (0,)), ((), ())), preferred_element_type=f32)


def dot(a, b):
    return lax.dot_general(a, b, (((1,), (0,)), ((), ())), preferred_element_type=f32)


def halves(a):
    high = a.astype(bf16)
    return high, (a - high.astype(f32)).astype(bf16)


def fine(product, a, b):
    (a_high, a_low), (b_high, b_low) = halves(a), halves(b)
    return product(a_high, b_high) + (product(a_high, b_low) + product(a_low, b_high))


def fine_t(a, b):
    return fine(dot_t, a, b)


def fine_dot(a, b):
    return fine(dot, a, b)


def dot_r(a, b):
    return lax.dot_general(a, b, (((1,), (1,)), ((), ())), preferred_element_type=f32)


def in_hbm(array):
    return pltpu.with_memory_space_constraint(array, pltpu.HBM)


def whole():
    return pl.BlockSpec(memory_space=pltpu.VMEM)


def anywhere():
    return pl.BlockSpec(memory_space=pl.ANY)


def scalars():
    return pl.BlockSpec(memory_space=pltpu.SMEM)


def params(mib, semantics=None):
    return pltpu.CompilerParams(vmem_limit_bytes=mib << 20, dimension_semantics=semantics)


def cost(flops, nbytes):
    return pl.CostEstimate(flops=flops, bytes_accessed=nbytes, transcendentals=0)


def coefs_kernel(parent, sources, bases, up, root, leaf_out, root_out, held, basis, up_held, root_held, clusters, sems, tail_sems):
    group = sems.shape[0]
    step = held.shape[0] // group
    copies = []
    for part in range(group):
        rows = pl.ds(part * step, step)
        copies.append(pltpu.make_async_copy(sources.at[rows], held.at[rows], sems.at[part, 0]))
        copies.append(pltpu.make_async_copy(bases.at[rows], basis.at[rows], sems.at[part, 1]))
    tails = [
        pltpu.make_async_copy(up, up_held, tail_sems.at[0]),
        pltpu.make_async_copy(root, root_held, tail_sems.at[1]),
    ]
    for copy in copies + tails:
        copy.start()
    clusters[...] = jnp.zeros_like(clusters)
    exact = []
    for part in range(group):
        copies[2 * part].wait()
        copies[2 * part + 1].wait()
        for leaf in range(part * step, (part + 1) * step):
            exact.append(dot(basis[leaf], held[leaf]))
            leaf_out[leaf] = exact[leaf].astype(bf16)
    for tail in tails:
        tail.wait()
    for leaf, coefs in enumerate(exact):
        clusters[lax.rem(parent[leaf], clusters.shape[0])] += fine_t(up_held[leaf], coefs)
    total = fine_t(root_held[0], clusters[0])
    for cluster in range(1, root_held.shape[0]):
        total = total + fine_t(root_held[cluster], clusters[cluster])
    root_out[...] = total


def leaf_coefficients(leaf_parent, panels, bases, up_transfer, root_transfer):
    leaves, size, rhs = panels.shape
    rank = bases.shape[1]
    return pl.pallas_call(
        coefs_kernel,
        out_shape=(
            jax.ShapeDtypeStruct((leaves, rank, rhs), bf16),
            jax.ShapeDtypeStruct((rank, rhs), f32),
        ),
        in_specs=[scalars()] + [anywhere()] * 4,
        out_specs=(whole(), whole()),
        scratch_shapes=[
            pltpu.VMEM((leaves, size, rhs), bf16),
            pltpu.VMEM((leaves, rank, size), bf16),
            pltpu.VMEM(up_transfer.shape, f32),
            pltpu.VMEM(root_transfer.shape, f32),
            pltpu.VMEM((root_transfer.shape[0], rank, rhs), f32),
            pltpu.SemaphoreType.DMA((4, 2)),
            pltpu.SemaphoreType.DMA((2,)),
        ],
        compiler_params=params(12),
        cost_estimate=cost(1000, 1000),
        name="coefs",
    )(leaf_parent, *[in_hbm(array) for array in (panels, bases, up_transfer, root_transfer)])


def tables_kernel(nodes, transfer, coupling, transfer_out, coupling_out, held, sems):
    parts = sems.shape[1]
    step = held.shape[1] // parts
    rank, size = held.shape[2:]
    ids = lax.broadcasted_iota(jnp.int32, (nodes.shape[0], size), 1)
    chosen = (ids == nodes[...]).astype(bf16)
    copies = []
    for kind, table in enumerate((transfer, coupling)):
        for part in range(parts):
            rows = pl.ds(part * step, step)
            copies.append(pltpu.make_async_copy(table.at[rows], held.at[kind, rows], sems.at[kind, part]))
    for copy in copies:
        copy.start()
    for kind, out in enumerate((transfer_out, coupling_out)):
        for part in range(parts):
            copies[kind * parts + part].wait()
            first = part * step
            values = held[kind, first : first + step].reshape(-1, size)
            high = values.astype(bf16)
            low = (values - high.astype(f32)).astype(bf16)
            rows = dot_r(chosen, high) + dot_r(chosen, low)
            for row in range(step):
                out[:, first + row, :] = rows[:, row * rank : (row + 1) * rank]


def tables(nodes, transfer, coupling):
    count = nodes.shape[0]
    size, rank, _ = transfer.shape
    return pl.pallas_call(
        tables_kernel,
        out_shape=(jax.ShapeDtypeStruct((count, rank, rank), f32),) * 2,
        in_specs=[whole(), anywhere(), anywhere()],
        out_specs=(whole(),) * 2,
        scratch_shapes=[pltpu.VMEM((2, rank, rank, size), f32), pltpu.SemaphoreType.DMA((2, 8))],
        compiler_params=params(20),
        cost_estimate=cost(1000, 1000),
        name="tables",
    )(nodes, in_hbm(transfer.transpose(1, 2, 0)), in_hbm(coupling.transpose(1, 2, 0)))


def combine_kernel(own, other, current, sibling, mats, out):
    total = fine_t(mats[own], current[...])
    out[...] = total + fine_t(mats[other], sibling[...])


def combine(own, other, current, sibling, mats):
    return pl.pallas_call(
        lambda *refs: combine_kernel(own, other, *refs),
        out_shape=jax.ShapeDtypeStruct(current.shape, f32),
        in_specs=[whole(), whole(), whole()],
        out_specs=whole(),
        compiler_params=params(4),
        cost_estimate=cost(1000, 1000),
        name="combine",
    )(current, sibling, mats)


def combine_four_kernel(picks, root, one, two, three, mats, sibling_out, out):
    own, other, second, third, own_up, other_up = picks
    sibling = fine_t(mats[second], two[...]) + fine_t(mats[third], three[...])
    sibling_out[...] = sibling
    lower = fine_t(mats[own], root[...]) + fine_t(mats[other], one[...])
    out[...] = fine_t(mats[own_up], lower) + fine_t(mats[other_up], sibling)


def combine_four(picks, roots, mats):
    return pl.pallas_call(
        lambda *refs: combine_four_kernel(picks, *refs),
        out_shape=(jax.ShapeDtypeStruct(roots[0].shape, f32),) * 2,
        in_specs=[whole()] * 5,
        out_specs=(whole(),) * 2,
        compiler_params=params(2),
        cost_estimate=cost(1000, 1000),
        name="combine_four",
    )(*roots, mats)


def weights_kernel(count, coupling, out, held, sems):
    leaves, slots, _, rank = coupling.shape
    copies = [pltpu.make_async_copy(coupling.at[leaf], held.at[leaf], sems.at[leaf]) for leaf in range(leaves)]
    for copy in copies:
        copy.start()
    for leaf in range(leaves):
        used = count[leaf]
        copies[leaf].wait()
        for pair in range(slots // 2):
            left = jnp.where(2 * pair < used, held[leaf, 2 * pair], 0.0)
            right = jnp.where(2 * pair + 1 < used, held[leaf, 2 * pair + 1], 0.0)
            joined = jnp.concatenate([left, right], axis=1).astype(bf16)
            out[leaf, :, 2 * pair * rank : 2 * (pair + 1) * rank] = joined


def weights(far_count, far_coupling):
    leaves, slots, rank, _ = far_coupling.shape
    return pl.pallas_call(
        weights_kernel,
        out_shape=jax.ShapeDtypeStruct((leaves, rank, slots * rank), bf16),
        in_specs=[scalars(), anywhere()],
        out_specs=whole(),
        scratch_shapes=[pltpu.VMEM(far_coupling.shape, f32), pltpu.SemaphoreType.DMA((leaves,))],
        compiler_params=params(20),
        cost_estimate=cost(1000, 1000),
        name="weights",
    )(far_count, in_hbm(far_coupling))


def near_kernel(position, rows, packed, blocks, coefs, *refs):
    pieces = refs[:-10]
    out, far_out, held, matrices, table, piece_sems, block_sems, sums, out_sems, table_sem = refs[-10:]
    leaves, slots = blocks.shape[:2]
    far_slots = rows.shape[0] // leaves
    copies = []
    first = 0
    for index, piece in enumerate(pieces):
        span = pl.ds(first, piece.shape[0])
        copies.append(pltpu.make_async_copy(piece, held.at[span], piece_sems.at[index]))
        first += piece.shape[0]
    fetches = [
        pltpu.make_async_copy(blocks.at[leaf], matrices.at[leaf], block_sems.at[leaf]) for leaf in range(leaves)
    ]
    load = pltpu.make_async_copy(coefs, table, table_sem)
    load.start()
    for copy in copies + fetches[:1]:
        copy.start()
    load.wait()
    for leaf in range(leaves):
        tall = jnp.concatenate([table[rows[leaf * far_slots + slot]] for slot in range(far_slots)], axis=0)
        far_out[leaf] = dot(packed[leaf], tall)
    for copy in copies:
        copy.wait()
    for fetch in fetches[1:]:
        fetch.start()
    stores = []
    for leaf in range(leaves):
        fetches[leaf].wait()
        wide = jnp.concatenate([matrices[leaf, slot] for slot in range(slots)], axis=1)
        tall = jnp.concatenate([held[position[leaf * slots + slot]] for slot in range(slots)], axis=0)
        sums[leaf] = dot(wide, tall)
        stores.append(pltpu.make_async_copy(sums.at[leaf], out.at[leaf], out_sems.at[leaf]))
        stores[leaf].start()
    for store in stores:
        store.wait()


def near(position, far_rows, packed, near_blocks, slab_coefs, pieces):
    leaves, slots, size, _ = near_blocks.shape
    rank, rhs = slab_coefs.shape[1:]
    return pl.pallas_call(
        near_kernel,
        out_shape=(pltpu.HBM((leaves, size, rhs), f32), jax.ShapeDtypeStruct((leaves, rank, rhs), f32)),
        in_specs=[scalars(), scalars(), whole()] + [anywhere()] * (2 + len(pieces)),
        out_specs=(pl.BlockSpec(memory_space=pltpu.HBM), whole()),
        scratch_shapes=[
            pltpu.VMEM((sum(piece.shape[0] for piece in pieces), size, rhs), bf16),
            pltpu.VMEM(near_blocks.shape, bf16),
            pltpu.VMEM(slab_coefs.shape, bf16),
            pltpu.SemaphoreType.DMA((len(pieces),)),
            pltpu.SemaphoreType.DMA((leaves,)),
            pltpu.VMEM((leaves, size, rhs), f32),
            pltpu.SemaphoreType.DMA((leaves,)),
            pltpu.SemaphoreType.DMA,
        ],
        compiler_params=params(42),
        cost_estimate=cost(1000, 1000),
        name="near",
    )(position, far_rows, packed, in_hbm(near_blocks), in_hbm(slab_coefs), *pieces)


def final_kernel(depth, parent, *refs):
    siblings = refs[:depth]
    transfer, coupling, root, up, far_part, bases, near_part, out = refs[depth : depth + 8]
    clusters, results, basis, close, basis_sem, near_sems, out_sems = refs[depth + 8 :]
    leaves = up.shape[0]
    load = pltpu.make_async_copy(bases, basis, basis_sem)
    nears = [pltpu.make_async_copy(near_part.at[leaf], close.at[leaf], near_sems.at[leaf]) for leaf in range(leaves)]
    for copy in [load] + nears:
        copy.start()
    down = fine_dot(coupling[depth - 1], siblings[depth - 1][...])
    for level in reversed(range(depth - 1)):
        across = fine_dot(coupling[level], siblings[level][...])
        down = across + fine_dot(transfer[level], down)
    for cluster in range(root.shape[0]):
        clusters[cluster] = fine_dot(root[cluster], down)
    load.wait()
    stores = []
    for leaf in range(leaves):
        on_leaf = fine_dot(up[leaf], clusters[lax.rem(parent[leaf], root.shape[0])])
        expansion = (on_leaf + far_part[leaf]).astype(bf16)
        nears[leaf].wait()
        results[leaf] = (dot_t(basis[leaf], expansion) + close[leaf]).astype(bf16)
        stores.append(pltpu.make_async_copy(results.at[leaf], out.at[leaf], out_sems.at[leaf]))
        stores[leaf].start()
    for store in stores:
        store.wait()


def final(leaf_parent, siblings, transfer, coupling, root_transfer, up_transfer, far_part, bases, near_part):
    leaves, rank, size = bases.shape
    rhs = near_part.shape[2]
    depth = len(siblings)
    return pl.pallas_call(
        lambda *refs: final_kernel(depth, *refs),
        out_shape=jax.ShapeDtypeStruct((leaves, size, rhs), bf16),
        in_specs=[scalars()] + [whole()] * (depth + 5) + [anywhere()] * 2,
        out_specs=anywhere(),
        scratch_shapes=[
            pltpu.VMEM((root_transfer.shape[0], rank, rhs), f32),
            pltpu.VMEM((leaves, size, rhs), bf16),
            pltpu.VMEM(bases.shape, bf16),
            pltpu.VMEM(near_part.shape, f32),
            pltpu.SemaphoreType.DMA,
            pltpu.SemaphoreType.DMA((leaves,)),
            pltpu.SemaphoreType.DMA((leaves,)),
        ],
        compiler_params=params(12),
        cost_estimate=cost(1000, 1000),
        name="final",
    )(
        leaf_parent,
        *siblings,
        transfer,
        coupling,
        root_transfer,
        up_transfer,
        far_part,
        in_hbm(bases),
        in_hbm(near_part),
    )


def shifted(array, axis, step, closed):
    count = lax.axis_size(axis)
    pairs = [(i, (i + step) % count) for i in range(count) if closed or 0 <= i + step < count]
    return lax.ppermute(array, axis, pairs)


def both(array, axis, closed):
    return shifted(array, axis, 1, closed), shifted(array, axis, -1, closed)


def after(*arrays):
    return lax.optimization_barrier(arrays)


def partner(array, axis, flip):
    return lax.ppermute(array, axis, [(i, i ^ flip) for i in range(lax.axis_size(axis))])


def local(
    sources,
    bases,
    leaf_parent,
    up_transfer,
    root_transfer,
    top_transfer,
    top_coupling,
    near_list,
    near_blocks,
    far_list,
    far_count,
    far_coupling,
):
    leaf_total, leaf_size, _ = bases.shape
    bases = bases.transpose(0, 2, 1)
    rhs_count = sources.shape[1]
    slab_count = lax.axis_size("slab")
    sector_count = lax.axis_size("sector")
    devices = slab_count * sector_count
    depth = devices.bit_length() - 1
    slab_pos = lax.axis_index("slab")
    sector_pos = lax.axis_index("sector")
    device = slab_pos * sector_count + sector_pos
    panels = sources.reshape(leaf_total, leaf_size, rhs_count)

    leaf_coefs, root = leaf_coefficients(leaf_parent, panels, bases, up_transfer, root_transfer)
    slab_coefs = lax.all_gather(leaf_coefs, "sector", axis=0, tiled=True)

    owner_device = near_list // leaf_total
    slab_offset = (owner_device // sector_count - slab_pos) % 3
    sector_offset = (owner_device % sector_count - sector_pos) % sector_count
    row = jnp.where(sector_offset == 0, 0, jnp.where(sector_offset == 1, 6, 3)) + slab_offset
    position = (row * leaf_total + near_list % leaf_total).reshape(-1)
    far_rows = (far_list - slab_pos * (sector_count * leaf_total)).reshape(-1)

    both_axes = ("slab", "sector")
    sides = both(panels, "sector", True)
    slots = jnp.arange(2 * depth + 2, dtype=jnp.int32)
    level_of = jnp.where(slots < 2 * depth, slots % depth, 0)
    flips = jnp.where(slots < 2 * depth, slots // depth, 2 + slots % 2)
    nodes = ((devices + device) >> level_of) ^ flips
    transfer, coupling = tables(nodes[:, None], top_transfer, top_coupling)
    below, above = both(panels, "slab", False)
    packed = weights(far_count, far_coupling)

    root, below, above, packed, transfer, position, far_rows = after(
        root, below, above, packed, transfer, position, far_rows
    )
    quad = [root] + [partner(root, both_axes, flip) for flip in (1, 2, 3)]
    flat = after(*quad, *sides)
    quad, sides = flat[:4], flat[4:]
    corners = [both(side, "slab", False) for side in sides]
    pieces = [in_hbm(panels), above, below]
    for side, corner in zip(sides, corners):
        pieces += [side, corner[1], corner[0]]
    picks = (0, depth, 2 * depth, 2 * depth + 1, 1, depth + 1)
    across, current = combine_four(picks, quad, transfer)
    siblings = [quad[1], across]
    for level in range(2, depth):
        if level == depth - 1:
            current, slab_coefs = after(current, slab_coefs)
        sibling = partner(current, both_axes, 1 << level)
        if level == depth - 1:
            near_part, far_part = near(position, far_rows, packed, near_blocks, slab_coefs, pieces)
            sibling, near_part, far_part = after(sibling, near_part, far_part)
        siblings.append(sibling)
        if level < depth - 1:
            current = combine(level, depth + level, current, sibling, transfer)
    field = final(
        leaf_parent, siblings, transfer, coupling, root_transfer, up_transfer, far_part, bases, near_part
    )
    return field.reshape(leaf_total * leaf_size, rhs_count)


def solution(mesh):
    placed = (
        P(("slab", "sector"), None),
        P(("slab", "sector"), None, None),
        P(("slab", "sector")),
        P(("slab", "sector"), None, None),
        P(("slab", "sector"), None, None),
        P(),
        P(),
        P(("slab", "sector"), None),
        P(("slab", "sector"), None, None, None),
        P(("slab", "sector"), None),
        P(("slab", "sector")),
        P(("slab", "sector"), None, None, None),
    )
    return jax.shard_map(
        local, mesh=mesh, in_specs=placed, out_specs=P(("slab", "sector"), None), check_vma=False
    )
```

```python
import jax
import jax.numpy as jnp
from jax import lax
from jax.experimental import pallas as pl
from jax.experimental.pallas import tpu as pltpu
from jax.sharding import PartitionSpec as P

f32 = jnp.float32
bf16 = jnp.bfloat16


def dot_t(a, b):
    return lax.dot_general(a, b, (((0,), (0,)), ((), ())), preferred_element_type=f32)


def dot(a, b):
    return lax.dot_general(a, b, (((1,), (0,)), ((), ())), preferred_element_type=f32)


def halves(a):
    high = a.astype(bf16)
    return high, (a - high.astype(f32)).astype(bf16)


def fine(product, a, b):
    (a_high, a_low), (b_high, b_low) = halves(a), halves(b)
    return product(a_high, b_high) + (product(a_high, b_low) + product(a_low, b_high))


def fine_t(a, b):
    return fine(dot_t, a, b)


def fine_dot(a, b):
    return fine(dot, a, b)


def dot_r(a, b):
    return lax.dot_general(a, b, (((1,), (1,)), ((), ())), preferred_element_type=f32)


def in_hbm(array):
    return pltpu.with_memory_space_constraint(array, pltpu.HBM)


def whole():
    return pl.BlockSpec(memory_space=pltpu.VMEM)


def anywhere():
    return pl.BlockSpec(memory_space=pl.ANY)


def scalars():
    return pl.BlockSpec(memory_space=pltpu.SMEM)


def params(mib, semantics=None):
    return pltpu.CompilerParams(vmem_limit_bytes=mib << 20, dimension_semantics=semantics)


def cost(flops, nbytes):
    return pl.CostEstimate(flops=flops, bytes_accessed=nbytes, transcendentals=0)


def coefs_kernel(parent, sources, bases, up, root, leaf_out, root_out, held, basis, up_held, root_held, clusters, sems, tail_sems):
    group = sems.shape[0]
    step = held.shape[0] // group
    copies = []
    for part in range(group):
        rows = pl.ds(part * step, step)
        copies.append(pltpu.make_async_copy(sources.at[rows], held.at[rows], sems.at[part, 0]))
        copies.append(pltpu.make_async_copy(bases.at[rows], basis.at[rows], sems.at[part, 1]))
    tails = [
        pltpu.make_async_copy(up, up_held, tail_sems.at[0]),
        pltpu.make_async_copy(root, root_held, tail_sems.at[1]),
    ]
    for copy in copies + tails:
        copy.start()
    clusters[...] = jnp.zeros_like(clusters)
    exact = []
    for part in range(group):
        copies[2 * part].wait()
        copies[2 * part + 1].wait()
        for leaf in range(part * step, (part + 1) * step):
            exact.append(dot(basis[leaf], held[leaf]))
            leaf_out[leaf] = exact[leaf].astype(bf16)
    for tail in tails:
        tail.wait()
    for leaf, coefs in enumerate(exact):
        clusters[lax.rem(parent[leaf], clusters.shape[0])] += fine_t(up_held[leaf], coefs)
    total = fine_t(root_held[0], clusters[0])
    for cluster in range(1, root_held.shape[0]):
        total = total + fine_t(root_held[cluster], clusters[cluster])
    root_out[...] = total


def leaf_coefficients(leaf_parent, panels, bases, up_transfer, root_transfer):
    leaves, size, rhs = panels.shape
    rank = bases.shape[1]
    return pl.pallas_call(
        coefs_kernel,
        out_shape=(
            jax.ShapeDtypeStruct((leaves, rank, rhs), bf16),
            jax.ShapeDtypeStruct((rank, rhs), f32),
        ),
        in_specs=[scalars()] + [anywhere()] * 4,
        out_specs=(whole(), whole()),
        scratch_shapes=[
            pltpu.VMEM((leaves, size, rhs), bf16),
            pltpu.VMEM((leaves, rank, size), bf16),
            pltpu.VMEM(up_transfer.shape, f32),
            pltpu.VMEM(root_transfer.shape, f32),
            pltpu.VMEM((root_transfer.shape[0], rank, rhs), f32),
            pltpu.SemaphoreType.DMA((4, 2)),
            pltpu.SemaphoreType.DMA((2,)),
        ],
        compiler_params=params(12),
        cost_estimate=cost(1000, 1000),
        name="coefs",
    )(leaf_parent, *[in_hbm(array) for array in (panels, bases, up_transfer, root_transfer)])


def tables_kernel(nodes, transfer, coupling, transfer_out, coupling_out, held, sems):
    parts = sems.shape[1]
    step = held.shape[1] // parts
    rank, size = held.shape[2:]
    ids = lax.broadcasted_iota(jnp.int32, (nodes.shape[0], size), 1)
    chosen = (ids == nodes[...]).astype(bf16)
    copies = []
    for kind, table in enumerate((transfer, coupling)):
        for part in range(parts):
            rows = pl.ds(part * step, step)
            copies.append(pltpu.make_async_copy(table.at[rows], held.at[kind, rows], sems.at[kind, part]))
    for copy in copies:
        copy.start()
    for kind, out in enumerate((transfer_out, coupling_out)):
        for part in range(parts):
            copies[kind * parts + part].wait()
            first = part * step
            values = held[kind, first : first + step].reshape(-1, size)
            high = values.astype(bf16)
            low = (values - high.astype(f32)).astype(bf16)
            rows = dot_r(chosen, high) + dot_r(chosen, low)
            for row in range(step):
                out[:, first + row, :] = rows[:, row * rank : (row + 1) * rank]


def tables(nodes, transfer, coupling):
    count = nodes.shape[0]
    size, rank, _ = transfer.shape
    return pl.pallas_call(
        tables_kernel,
        out_shape=(jax.ShapeDtypeStruct((count, rank, rank), f32),) * 2,
        in_specs=[whole(), anywhere(), anywhere()],
        out_specs=(whole(),) * 2,
        scratch_shapes=[pltpu.VMEM((2, rank, rank, size), f32), pltpu.SemaphoreType.DMA((2, 8))],
        compiler_params=params(20),
        cost_estimate=cost(1000, 1000),
        name="tables",
    )(nodes, in_hbm(transfer.transpose(1, 2, 0)), in_hbm(coupling.transpose(1, 2, 0)))


def combine_kernel(own, other, current, sibling, mats, out):
    total = fine_t(mats[own], current[...])
    out[...] = total + fine_t(mats[other], sibling[...])


def combine(own, other, current, sibling, mats):
    return pl.pallas_call(
        lambda *refs: combine_kernel(own, other, *refs),
        out_shape=jax.ShapeDtypeStruct(current.shape, f32),
        in_specs=[whole(), whole(), whole()],
        out_specs=whole(),
        compiler_params=params(4),
        cost_estimate=cost(1000, 1000),
        name="combine",
    )(current, sibling, mats)


def combine_four_kernel(picks, root, one, two, three, mats, sibling_out, out):
    own, other, second, third, own_up, other_up = picks
    sibling = fine_t(mats[second], two[...]) + fine_t(mats[third], three[...])
    sibling_out[...] = sibling
    lower = fine_t(mats[own], root[...]) + fine_t(mats[other], one[...])
    out[...] = fine_t(mats[own_up], lower) + fine_t(mats[other_up], sibling)


def combine_four(picks, roots, mats):
    return pl.pallas_call(
        lambda *refs: combine_four_kernel(picks, *refs),
        out_shape=(jax.ShapeDtypeStruct(roots[0].shape, f32),) * 2,
        in_specs=[whole()] * 5,
        out_specs=(whole(),) * 2,
        compiler_params=params(2),
        cost_estimate=cost(1000, 1000),
        name="combine_four",
    )(*roots, mats)


def downward_kernel(depth, parent, *refs):
    siblings = refs[:depth]
    transfer, coupling, root, up, out, clusters = refs[depth:]
    down = fine_dot(coupling[depth - 1], siblings[depth - 1][...])
    for level in reversed(range(depth - 1)):
        across = fine_dot(coupling[level], siblings[level][...])
        down = across + fine_dot(transfer[level], down)
    for cluster in range(root.shape[0]):
        clusters[cluster] = fine_dot(root[cluster], down)
    for leaf in range(up.shape[0]):
        out[leaf] = fine_dot(up[leaf], clusters[lax.rem(parent[leaf], root.shape[0])])


def downward(leaf_parent, siblings, transfer, coupling, root_transfer, up_transfer):
    depth = len(siblings)
    rank, rhs = siblings[0].shape
    return pl.pallas_call(
        lambda *refs: downward_kernel(depth, *refs),
        out_shape=jax.ShapeDtypeStruct((up_transfer.shape[0], rank, rhs), f32),
        in_specs=[scalars()] + [whole()] * (depth + 4),
        out_specs=whole(),
        scratch_shapes=[pltpu.VMEM((root_transfer.shape[0], rank, rhs), f32)],
        compiler_params=params(16),
        cost_estimate=cost(1000, 1000),
        name="downward",
    )(leaf_parent, *siblings, transfer, coupling, root_transfer, up_transfer)


def weights_kernel(count, coupling, bases, out, upright, held, basis, sems, basis_sem):
    leaves, slots, _, rank = coupling.shape
    load = pltpu.make_async_copy(bases, basis, basis_sem)
    copies = [pltpu.make_async_copy(coupling.at[leaf], held.at[leaf], sems.at[leaf]) for leaf in range(leaves)]
    for copy in [load] + copies:
        copy.start()
    rows = lax.broadcasted_iota(jnp.int32, (rank, rank), 0)
    unit = (rows == lax.broadcasted_iota(jnp.int32, (rank, rank), 1)).astype(bf16)
    load.wait()
    for leaf in range(leaves):
        upright[leaf] = dot_t(basis[leaf], unit).astype(bf16)
    for leaf in range(leaves):
        used = count[leaf]
        copies[leaf].wait()
        for pair in range(slots // 2):
            left = jnp.where(2 * pair < used, held[leaf, 2 * pair], 0.0)
            right = jnp.where(2 * pair + 1 < used, held[leaf, 2 * pair + 1], 0.0)
            joined = jnp.concatenate([left, right], axis=1).astype(bf16)
            out[leaf, :, 2 * pair * rank : 2 * (pair + 1) * rank] = joined


def weights(far_count, far_coupling, bases):
    leaves, slots, rank, _ = far_coupling.shape
    size = bases.shape[2]
    return pl.pallas_call(
        weights_kernel,
        out_shape=(
            jax.ShapeDtypeStruct((leaves, rank, slots * rank), bf16),
            jax.ShapeDtypeStruct((leaves, size, rank), bf16),
        ),
        in_specs=[scalars(), anywhere(), anywhere()],
        out_specs=(whole(), whole()),
        scratch_shapes=[
            pltpu.VMEM(far_coupling.shape, f32),
            pltpu.VMEM(bases.shape, bf16),
            pltpu.SemaphoreType.DMA((leaves,)),
            pltpu.SemaphoreType.DMA,
        ],
        compiler_params=params(20),
        cost_estimate=cost(1000, 1000),
        name="weights",
    )(far_count, in_hbm(far_coupling), in_hbm(bases))


def near_kernel(position, blocks, *refs):
    pieces = refs[:-7]
    out, held, matrices, piece_sems, block_sems, sums, out_sems = refs[-7:]
    leaves, slots = blocks.shape[:2]
    copies = []
    first = 0
    for index, piece in enumerate(pieces):
        rows = pl.ds(first, piece.shape[0])
        copies.append(pltpu.make_async_copy(piece, held.at[rows], piece_sems.at[index]))
        first += piece.shape[0]
    fetches = [
        pltpu.make_async_copy(blocks.at[leaf], matrices.at[leaf], block_sems.at[leaf]) for leaf in range(leaves)
    ]
    for copy in copies + fetches[:1]:
        copy.start()
    for copy in copies:
        copy.wait()
    for fetch in fetches[1:]:
        fetch.start()
    stores = []
    for leaf in range(leaves):
        fetches[leaf].wait()
        wide = jnp.concatenate([matrices[leaf, slot] for slot in range(slots)], axis=1)
        tall = jnp.concatenate([held[position[leaf * slots + slot]] for slot in range(slots)], axis=0)
        sums[leaf] = dot(wide, tall)
        stores.append(pltpu.make_async_copy(sums.at[leaf], out.at[leaf], out_sems.at[leaf]))
        stores[leaf].start()
    for store in stores:
        store.wait()


def near(position, near_blocks, pieces):
    leaves, slots, size, _ = near_blocks.shape
    rhs = pieces[0].shape[2]
    return pl.pallas_call(
        near_kernel,
        out_shape=pltpu.HBM((leaves, size, rhs), f32),
        in_specs=[scalars()] + [anywhere()] * (1 + len(pieces)),
        out_specs=pl.BlockSpec(memory_space=pltpu.HBM),
        scratch_shapes=[
            pltpu.VMEM((sum(piece.shape[0] for piece in pieces), size, rhs), bf16),
            pltpu.VMEM(near_blocks.shape, bf16),
            pltpu.SemaphoreType.DMA((len(pieces),)),
            pltpu.SemaphoreType.DMA((leaves,)),
            pltpu.VMEM((leaves, size, rhs), f32),
            pltpu.SemaphoreType.DMA((leaves,)),
        ],
        compiler_params=params(36),
        cost_estimate=cost(1000, 1000),
        name="near",
    )(position, in_hbm(near_blocks), *pieces)


def final_kernel(rows, packed, coefs, on_leaf, bases, near_part, out, *scratch):
    held, results, term, basis, close, load_sems, near_sems, out_sems = scratch
    leaves, rank, wide = packed.shape
    slots = wide // rank
    loads = [
        pltpu.make_async_copy(source, target, load_sems.at[index])
        for index, (source, target) in enumerate(((coefs, held), (on_leaf, term), (bases, basis)))
    ]
    nears = [pltpu.make_async_copy(near_part.at[leaf], close.at[leaf], near_sems.at[leaf]) for leaf in range(leaves)]
    for load in loads:
        load.start()
    for load in loads:
        load.wait()
    for load in nears:
        load.start()
    stores = []
    for leaf in range(leaves):
        tall = jnp.concatenate([held[rows[leaf * slots + slot]] for slot in range(slots)], axis=0)
        expansion = (term[leaf] + dot(packed[leaf], tall)).astype(bf16)
        nears[leaf].wait()
        results[leaf] = (dot(basis[leaf], expansion) + close[leaf]).astype(bf16)
        stores.append(pltpu.make_async_copy(results.at[leaf], out.at[leaf], out_sems.at[leaf]))
        stores[leaf].start()
    for store in stores:
        store.wait()


def final(far_rows, packed, slab_coefs, on_leaf, bases, near_part):
    leaves, size, rank = bases.shape
    rhs = near_part.shape[2]
    return pl.pallas_call(
        final_kernel,
        out_shape=jax.ShapeDtypeStruct((leaves, size, rhs), bf16),
        in_specs=[scalars(), whole()] + [anywhere()] * 4,
        out_specs=anywhere(),
        scratch_shapes=[
            pltpu.VMEM(slab_coefs.shape, bf16),
            pltpu.VMEM((leaves, size, rhs), bf16),
            pltpu.VMEM(on_leaf.shape, f32),
            pltpu.VMEM(bases.shape, bf16),
            pltpu.VMEM(near_part.shape, f32),
            pltpu.SemaphoreType.DMA((3,)),
            pltpu.SemaphoreType.DMA((leaves,)),
            pltpu.SemaphoreType.DMA((leaves,)),
        ],
        compiler_params=params(24),
        cost_estimate=cost(1000, 1000),
        name="final",
    )(far_rows, packed, in_hbm(slab_coefs), on_leaf, in_hbm(bases), in_hbm(near_part))


def shifted(array, axis, step, closed):
    count = lax.axis_size(axis)
    pairs = [(i, (i + step) % count) for i in range(count) if closed or 0 <= i + step < count]
    return lax.ppermute(array, axis, pairs)


def both(array, axis, closed):
    return shifted(array, axis, 1, closed), shifted(array, axis, -1, closed)


def after(*arrays):
    return lax.optimization_barrier(arrays)


def partner(array, axis, flip):
    return lax.ppermute(array, axis, [(i, i ^ flip) for i in range(lax.axis_size(axis))])


def local(
    sources,
    bases,
    leaf_parent,
    up_transfer,
    root_transfer,
    top_transfer,
    top_coupling,
    near_list,
    near_blocks,
    far_list,
    far_count,
    far_coupling,
):
    leaf_total, leaf_size, _ = bases.shape
    bases = bases.transpose(0, 2, 1)
    rhs_count = sources.shape[1]
    slab_count = lax.axis_size("slab")
    sector_count = lax.axis_size("sector")
    devices = slab_count * sector_count
    depth = devices.bit_length() - 1
    slab_pos = lax.axis_index("slab")
    sector_pos = lax.axis_index("sector")
    device = slab_pos * sector_count + sector_pos
    panels = sources.reshape(leaf_total, leaf_size, rhs_count)

    leaf_coefs, root = leaf_coefficients(leaf_parent, panels, bases, up_transfer, root_transfer)
    slab_coefs = lax.all_gather(leaf_coefs, "sector", axis=0, tiled=True)

    owner_device = near_list // leaf_total
    slab_offset = (owner_device // sector_count - slab_pos) % 3
    sector_offset = (owner_device % sector_count - sector_pos) % sector_count
    row = jnp.where(sector_offset == 0, 0, jnp.where(sector_offset == 1, 6, 3)) + slab_offset
    position = (row * leaf_total + near_list % leaf_total).reshape(-1)
    far_rows = (far_list - slab_pos * (sector_count * leaf_total)).reshape(-1)

    both_axes = ("slab", "sector")
    sides = both(panels, "sector", True)
    slots = jnp.arange(2 * depth + 2, dtype=jnp.int32)
    level_of = jnp.where(slots < 2 * depth, slots % depth, 0)
    flips = jnp.where(slots < 2 * depth, slots // depth, 2 + slots % 2)
    nodes = ((devices + device) >> level_of) ^ flips
    transfer, coupling = tables(nodes[:, None], top_transfer, top_coupling)
    below, above = both(panels, "slab", False)
    packed, upright = weights(far_count, far_coupling, bases)

    root, below, above, packed, upright, transfer, position, far_rows = after(
        root, below, above, packed, upright, transfer, position, far_rows
    )
    quad = [root] + [partner(root, both_axes, flip) for flip in (1, 2, 3)]
    flat = after(*quad, *sides)
    quad, sides = flat[:4], flat[4:]
    corners = [both(side, "slab", False) for side in sides]
    pieces = [in_hbm(panels), above, below]
    for side, corner in zip(sides, corners):
        pieces += [side, corner[1], corner[0]]
    picks = (0, depth, 2 * depth, 2 * depth + 1, 1, depth + 1)
    across, current = combine_four(picks, quad, transfer)
    siblings = [quad[1], across]
    for level in range(2, depth):
        sibling = partner(current, both_axes, 1 << level)
        if level == depth - 1:
            near_part = near(position, near_blocks, pieces)
            current, sibling, near_part = after(current, sibling, near_part)
        siblings.append(sibling)
        if level < depth - 1:
            current = combine(level, depth + level, current, sibling, transfer)
    on_leaf = downward(leaf_parent, siblings, transfer, coupling, root_transfer, up_transfer)
    field = final(far_rows, packed, slab_coefs, on_leaf, upright, near_part)
    return field.reshape(leaf_total * leaf_size, rhs_count)


def solution(mesh):
    placed = (
        P(("slab", "sector"), None),
        P(("slab", "sector"), None, None),
        P(("slab", "sector")),
        P(("slab", "sector"), None, None),
        P(("slab", "sector"), None, None),
        P(),
        P(),
        P(("slab", "sector"), None),
        P(("slab", "sector"), None, None, None),
        P(("slab", "sector"), None),
        P(("slab", "sector")),
        P(("slab", "sector"), None, None, None),
    )
    return jax.shard_map(
        local, mesh=mesh, in_specs=placed, out_specs=P(("slab", "sector"), None), check_vma=False
    )
```

```python
import jax
import jax.numpy as jnp
from jax import lax
from jax.experimental import pallas as pl
from jax.experimental.pallas import tpu as pltpu
from jax.sharding import PartitionSpec as P

f32 = jnp.float32
bf16 = jnp.bfloat16


def dot_t(a, b):
    return lax.dot_general(a, b, (((0,), (0,)), ((), ())), preferred_element_type=f32)


def dot(a, b):
    return lax.dot_general(a, b, (((1,), (0,)), ((), ())), preferred_element_type=f32)


def halves(a):
    high = a.astype(bf16)
    return high, (a - high.astype(f32)).astype(bf16)


def fine(product, a, b):
    (a_high, a_low), (b_high, b_low) = halves(a), halves(b)
    return product(a_high, b_high) + (product(a_high, b_low) + product(a_low, b_high))


def fine_t(a, b):
    return fine(dot_t, a, b)


def fine_dot(a, b):
    return fine(dot, a, b)


def dot_r(a, b):
    return lax.dot_general(a, b, (((1,), (1,)), ((), ())), preferred_element_type=f32)


def in_hbm(array):
    return pltpu.with_memory_space_constraint(array, pltpu.HBM)


def whole():
    return pl.BlockSpec(memory_space=pltpu.VMEM)


def anywhere():
    return pl.BlockSpec(memory_space=pl.ANY)


def scalars():
    return pl.BlockSpec(memory_space=pltpu.SMEM)


def params(mib, semantics=None):
    return pltpu.CompilerParams(vmem_limit_bytes=mib << 20, dimension_semantics=semantics)


def cost(flops, nbytes):
    return pl.CostEstimate(flops=flops, bytes_accessed=nbytes, transcendentals=0)


def coefs_kernel(parent, sources, bases, up, root, leaf_out, root_out, held, basis, up_held, root_held, clusters, sems, tail_sems):
    group = sems.shape[0]
    step = held.shape[0] // group
    copies = []
    for part in range(group):
        rows = pl.ds(part * step, step)
        copies.append(pltpu.make_async_copy(sources.at[rows], held.at[rows], sems.at[part, 0]))
        copies.append(pltpu.make_async_copy(bases.at[rows], basis.at[rows], sems.at[part, 1]))
    tails = [
        pltpu.make_async_copy(up, up_held, tail_sems.at[0]),
        pltpu.make_async_copy(root, root_held, tail_sems.at[1]),
    ]
    for copy in copies + tails:
        copy.start()
    clusters[...] = jnp.zeros_like(clusters)
    exact = []
    for part in range(group):
        copies[2 * part].wait()
        copies[2 * part + 1].wait()
        for leaf in range(part * step, (part + 1) * step):
            exact.append(dot(basis[leaf], held[leaf]))
            leaf_out[leaf] = exact[leaf].astype(bf16)
    for tail in tails:
        tail.wait()
    for leaf, coefs in enumerate(exact):
        clusters[parent[leaf]] += fine_t(up_held[leaf], coefs)
    total = fine_t(root_held[0], clusters[0])
    for cluster in range(1, root_held.shape[0]):
        total = total + fine_t(root_held[cluster], clusters[cluster])
    root_out[...] = total


def leaf_coefficients(local_parent, panels, bases, up_transfer, root_transfer):
    leaves, size, rhs = panels.shape
    rank = bases.shape[1]
    return pl.pallas_call(
        coefs_kernel,
        out_shape=(
            jax.ShapeDtypeStruct((leaves, rank, rhs), bf16),
            jax.ShapeDtypeStruct((rank, rhs), f32),
        ),
        in_specs=[scalars()] + [anywhere()] * 4,
        out_specs=(whole(), whole()),
        scratch_shapes=[
            pltpu.VMEM((leaves, size, rhs), bf16),
            pltpu.VMEM((leaves, rank, size), bf16),
            pltpu.VMEM(up_transfer.shape, f32),
            pltpu.VMEM(root_transfer.shape, f32),
            pltpu.VMEM((root_transfer.shape[0], rank, rhs), f32),
            pltpu.SemaphoreType.DMA((4, 2)),
            pltpu.SemaphoreType.DMA((2,)),
        ],
        compiler_params=params(12),
        cost_estimate=cost(1000, 1000),
        name="coefs",
    )(local_parent, *[in_hbm(array) for array in (panels, bases, up_transfer, root_transfer)])


def tables_kernel(nodes, transfer, coupling, transfer_out, coupling_out, held, sems):
    parts = sems.shape[1]
    step = held.shape[1] // parts
    rank, size = held.shape[2:]
    ids = lax.broadcasted_iota(jnp.int32, (nodes.shape[0], size), 1)
    chosen = (ids == nodes[...]).astype(bf16)
    copies = []
    for kind, table in enumerate((transfer, coupling)):
        for part in range(parts):
            rows = pl.ds(part * step, step)
            copies.append(pltpu.make_async_copy(table.at[rows], held.at[kind, rows], sems.at[kind, part]))
    for copy in copies:
        copy.start()
    for kind, out in enumerate((transfer_out, coupling_out)):
        for part in range(parts):
            copies[kind * parts + part].wait()
            first = part * step
            values = held[kind, first : first + step].reshape(-1, size)
            high = values.astype(bf16)
            low = (values - high.astype(f32)).astype(bf16)
            rows = dot_r(chosen, high) + dot_r(chosen, low)
            for row in range(step):
                out[:, first + row, :] = rows[:, row * rank : (row + 1) * rank]


def tables(nodes, transfer, coupling):
    count = nodes.shape[0]
    size, rank, _ = transfer.shape
    return pl.pallas_call(
        tables_kernel,
        out_shape=(jax.ShapeDtypeStruct((count, rank, rank), f32),) * 2,
        in_specs=[whole(), anywhere(), anywhere()],
        out_specs=(whole(),) * 2,
        scratch_shapes=[pltpu.VMEM((2, rank, rank, size), f32), pltpu.SemaphoreType.DMA((2, 8))],
        compiler_params=params(20),
        cost_estimate=cost(1000, 1000),
        name="tables",
    )(nodes, in_hbm(transfer.transpose(1, 2, 0)), in_hbm(coupling.transpose(1, 2, 0)))


def combine_kernel(own, other, current, sibling, mats, out):
    total = fine_t(mats[own], current[...])
    out[...] = total + fine_t(mats[other], sibling[...])


def combine(own, other, current, sibling, mats):
    return pl.pallas_call(
        lambda *refs: combine_kernel(own, other, *refs),
        out_shape=jax.ShapeDtypeStruct(current.shape, f32),
        in_specs=[whole(), whole(), whole()],
        out_specs=whole(),
        compiler_params=params(4),
        cost_estimate=cost(1000, 1000),
        name="combine",
    )(current, sibling, mats)


def combine_four_kernel(picks, root, one, two, three, mats, sibling_out, out):
    own, other, second, third, own_up, other_up = picks
    sibling = fine_t(mats[second], two[...]) + fine_t(mats[third], three[...])
    sibling_out[...] = sibling
    lower = fine_t(mats[own], root[...]) + fine_t(mats[other], one[...])
    out[...] = fine_t(mats[own_up], lower) + fine_t(mats[other_up], sibling)


def combine_four(picks, roots, mats):
    return pl.pallas_call(
        lambda *refs: combine_four_kernel(picks, *refs),
        out_shape=(jax.ShapeDtypeStruct(roots[0].shape, f32),) * 2,
        in_specs=[whole()] * 5,
        out_specs=(whole(),) * 2,
        compiler_params=params(2),
        cost_estimate=cost(1000, 1000),
        name="combine_four",
    )(*roots, mats)


def downward_kernel(depth, parent, *refs):
    siblings = refs[:depth]
    transfer, coupling, root, up, out, clusters = refs[depth:]
    down = fine_dot(coupling[depth - 1], siblings[depth - 1][...])
    for level in reversed(range(depth - 1)):
        across = fine_dot(coupling[level], siblings[level][...])
        down = across + fine_dot(transfer[level], down)
    for cluster in range(root.shape[0]):
        clusters[cluster] = fine_dot(root[cluster], down)
    for leaf in range(up.shape[0]):
        out[leaf] = fine_dot(up[leaf], clusters[parent[leaf]])


def downward(local_parent, siblings, transfer, coupling, root_transfer, up_transfer):
    depth = len(siblings)
    rank, rhs = siblings[0].shape
    return pl.pallas_call(
        lambda *refs: downward_kernel(depth, *refs),
        out_shape=jax.ShapeDtypeStruct((up_transfer.shape[0], rank, rhs), f32),
        in_specs=[scalars()] + [whole()] * (depth + 4),
        out_specs=whole(),
        scratch_shapes=[pltpu.VMEM((root_transfer.shape[0], rank, rhs), f32)],
        compiler_params=params(16),
        cost_estimate=cost(1000, 1000),
        name="downward",
    )(local_parent, *siblings, transfer, coupling, root_transfer, up_transfer)


def weights_kernel(count, coupling, out, held, sems):
    leaves, slots, _, rank = coupling.shape
    copies = [pltpu.make_async_copy(coupling.at[leaf], held.at[leaf], sems.at[leaf]) for leaf in range(leaves)]
    for copy in copies:
        copy.start()
    for leaf in range(leaves):
        used = count[leaf]
        copies[leaf].wait()
        for pair in range(slots // 2):
            left = jnp.where(2 * pair < used, held[leaf, 2 * pair], 0.0)
            right = jnp.where(2 * pair + 1 < used, held[leaf, 2 * pair + 1], 0.0)
            joined = jnp.concatenate([left, right], axis=1).astype(bf16)
            out[leaf, :, 2 * pair * rank : 2 * (pair + 1) * rank] = joined


def weights(far_count, far_coupling):
    leaves, slots, rank, _ = far_coupling.shape
    return pl.pallas_call(
        weights_kernel,
        out_shape=jax.ShapeDtypeStruct((leaves, rank, slots * rank), bf16),
        in_specs=[scalars(), anywhere()],
        out_specs=whole(),
        scratch_shapes=[pltpu.VMEM(far_coupling.shape, f32), pltpu.SemaphoreType.DMA((leaves,))],
        compiler_params=params(20),
        cost_estimate=cost(1000, 1000),
        name="weights",
    )(far_count, in_hbm(far_coupling))


def near_kernel(position, blocks, *refs):
    pieces = refs[:-7]
    out, held, matrices, piece_sems, block_sems, sums, out_sems = refs[-7:]
    leaves, slots = blocks.shape[:2]
    copies = []
    first = 0
    for index, piece in enumerate(pieces):
        rows = pl.ds(first, piece.shape[0])
        copies.append(pltpu.make_async_copy(piece, held.at[rows], piece_sems.at[index]))
        first += piece.shape[0]
    fetches = [
        pltpu.make_async_copy(blocks.at[leaf], matrices.at[leaf], block_sems.at[leaf]) for leaf in range(leaves)
    ]
    for copy in copies + fetches[:1]:
        copy.start()
    for copy in copies:
        copy.wait()
    for fetch in fetches[1:]:
        fetch.start()
    stores = []
    for leaf in range(leaves):
        fetches[leaf].wait()
        wide = jnp.concatenate([matrices[leaf, slot] for slot in range(slots)], axis=1)
        tall = jnp.concatenate([held[position[leaf * slots + slot]] for slot in range(slots)], axis=0)
        sums[leaf] = dot(wide, tall)
        stores.append(pltpu.make_async_copy(sums.at[leaf], out.at[leaf], out_sems.at[leaf]))
        stores[leaf].start()
    for store in stores:
        store.wait()


def near(position, near_blocks, pieces):
    leaves, slots, size, _ = near_blocks.shape
    rhs = pieces[0].shape[2]
    return pl.pallas_call(
        near_kernel,
        out_shape=pltpu.HBM((leaves, size, rhs), f32),
        in_specs=[scalars()] + [anywhere()] * (1 + len(pieces)),
        out_specs=pl.BlockSpec(memory_space=pltpu.HBM),
        scratch_shapes=[
            pltpu.VMEM((sum(piece.shape[0] for piece in pieces), size, rhs), bf16),
            pltpu.VMEM(near_blocks.shape, bf16),
            pltpu.SemaphoreType.DMA((len(pieces),)),
            pltpu.SemaphoreType.DMA((leaves,)),
            pltpu.VMEM((leaves, size, rhs), f32),
            pltpu.SemaphoreType.DMA((leaves,)),
        ],
        compiler_params=params(36),
        cost_estimate=cost(1000, 1000),
        name="near",
    )(position, in_hbm(near_blocks), *pieces)


def final_kernel(rows, packed, coefs, on_leaf, bases, near_part, out, *scratch):
    held, results, term, basis, close, load_sems, near_sems, out_sems = scratch
    leaves, rank, wide = packed.shape
    slots = wide // rank
    loads = [
        pltpu.make_async_copy(source, target, load_sems.at[index])
        for index, (source, target) in enumerate(((coefs, held), (on_leaf, term), (bases, basis)))
    ]
    nears = [pltpu.make_async_copy(near_part.at[leaf], close.at[leaf], near_sems.at[leaf]) for leaf in range(leaves)]
    for load in loads:
        load.start()
    for load in loads:
        load.wait()
    for load in nears:
        load.start()
    stores = []
    for leaf in range(leaves):
        tall = jnp.concatenate([held[rows[leaf * slots + slot]] for slot in range(slots)], axis=0)
        expansion = (term[leaf] + dot(packed[leaf], tall)).astype(bf16)
        nears[leaf].wait()
        results[leaf] = (dot_t(basis[leaf], expansion) + close[leaf]).astype(bf16)
        stores.append(pltpu.make_async_copy(results.at[leaf], out.at[leaf], out_sems.at[leaf]))
        stores[leaf].start()
    for store in stores:
        store.wait()


def final(far_rows, packed, slab_coefs, on_leaf, bases, near_part):
    leaves, rank, size = bases.shape
    rhs = near_part.shape[2]
    return pl.pallas_call(
        final_kernel,
        out_shape=jax.ShapeDtypeStruct((leaves, size, rhs), bf16),
        in_specs=[scalars(), whole()] + [anywhere()] * 4,
        out_specs=anywhere(),
        scratch_shapes=[
            pltpu.VMEM(slab_coefs.shape, bf16),
            pltpu.VMEM((leaves, size, rhs), bf16),
            pltpu.VMEM(on_leaf.shape, f32),
            pltpu.VMEM(bases.shape, bf16),
            pltpu.VMEM(near_part.shape, f32),
            pltpu.SemaphoreType.DMA((3,)),
            pltpu.SemaphoreType.DMA((leaves,)),
            pltpu.SemaphoreType.DMA((leaves,)),
        ],
        compiler_params=params(24),
        cost_estimate=cost(1000, 1000),
        name="final",
    )(far_rows, packed, in_hbm(slab_coefs), on_leaf, in_hbm(bases), in_hbm(near_part))


def shifted(array, axis, step, closed):
    count = lax.axis_size(axis)
    pairs = [(i, (i + step) % count) for i in range(count) if closed or 0 <= i + step < count]
    return lax.ppermute(array, axis, pairs)


def both(array, axis, closed):
    return shifted(array, axis, 1, closed), shifted(array, axis, -1, closed)


def after(*arrays):
    return lax.optimization_barrier(arrays)


def partner(array, axis, flip):
    return lax.ppermute(array, axis, [(i, i ^ flip) for i in range(lax.axis_size(axis))])


def local(
    sources,
    bases,
    leaf_parent,
    up_transfer,
    root_transfer,
    top_transfer,
    top_coupling,
    near_list,
    near_blocks,
    far_list,
    far_count,
    far_coupling,
):
    leaf_total, leaf_size, _ = bases.shape
    bases = bases.transpose(0, 2, 1)
    rhs_count = sources.shape[1]
    cluster_total = leaf_total // 2
    slab_count = lax.axis_size("slab")
    sector_count = lax.axis_size("sector")
    devices = slab_count * sector_count
    depth = devices.bit_length() - 1
    slab_pos = lax.axis_index("slab")
    sector_pos = lax.axis_index("sector")
    device = slab_pos * sector_count + sector_pos
    panels = sources.reshape(leaf_total, leaf_size, rhs_count)

    local_parent = leaf_parent - device * cluster_total
    leaf_coefs, root = leaf_coefficients(local_parent, panels, bases, up_transfer, root_transfer)
    slab_coefs = lax.all_gather(leaf_coefs, "sector", axis=0, tiled=True)

    owner_device = near_list // leaf_total
    slab_offset = (owner_device // sector_count - slab_pos) % 3
    sector_offset = (owner_device % sector_count - sector_pos) % sector_count
    row = jnp.where(sector_offset == 0, 0, jnp.where(sector_offset == 1, 6, 3)) + slab_offset
    position = (row * leaf_total + near_list % leaf_total).reshape(-1)
    far_rows = (far_list - slab_pos * (sector_count * leaf_total)).reshape(-1)

    both_axes = ("slab", "sector")
    sides = both(panels, "sector", True)
    slots = jnp.arange(2 * depth + 2, dtype=jnp.int32)
    level_of = jnp.where(slots < 2 * depth, slots % depth, 0)
    flips = jnp.where(slots < 2 * depth, slots // depth, 2 + slots % 2)
    nodes = ((devices + device) >> level_of) ^ flips
    transfer, coupling = tables(nodes[:, None], top_transfer, top_coupling)
    below, above = both(panels, "slab", False)
    packed = weights(far_count, far_coupling)

    root, below, above, packed, transfer, position, far_rows = after(
        root, below, above, packed, transfer, position, far_rows
    )
    quad = [root] + [partner(root, both_axes, flip) for flip in (1, 2, 3)]
    flat = after(*quad, *sides)
    quad, sides = flat[:4], flat[4:]
    corners = [both(side, "slab", False) for side in sides]
    pieces = [in_hbm(panels), above, below]
    for side, corner in zip(sides, corners):
        pieces += [side, corner[1], corner[0]]
    picks = (0, depth, 2 * depth, 2 * depth + 1, 1, depth + 1)
    across, current = combine_four(picks, quad, transfer)
    siblings = [quad[1], across]
    for level in range(2, depth):
        sibling = partner(current, both_axes, 1 << level)
        if level == depth - 1:
            near_part = near(position, near_blocks, pieces)
            current, sibling, near_part = after(current, sibling, near_part)
        siblings.append(sibling)
        if level < depth - 1:
            current = combine(level, depth + level, current, sibling, transfer)
    on_leaf = downward(local_parent, siblings, transfer, coupling, root_transfer, up_transfer)
    field = final(far_rows, packed, slab_coefs, on_leaf, bases, near_part)
    return field.reshape(leaf_total * leaf_size, rhs_count)


def solution(mesh):
    placed = (
        P(("slab", "sector"), None),
        P(("slab", "sector"), None, None),
        P(("slab", "sector")),
        P(("slab", "sector"), None, None),
        P(("slab", "sector"), None, None),
        P(),
        P(),
        P(("slab", "sector"), None),
        P(("slab", "sector"), None, None, None),
        P(("slab", "sector"), None),
        P(("slab", "sector")),
        P(("slab", "sector"), None, None, None),
    )
    return jax.shard_map(
        local, mesh=mesh, in_specs=placed, out_specs=P(("slab", "sector"), None), check_vma=False
    )
```
